256 devices in a mesh: subj: 32 (over z_hi, x, y), vert: 8 (over z_lo, core).
Axes of the slice: x: 4, y: 4, z: 8 (z_hi: 2, z_lo: 4; z = z_hi * 4 + z_lo), core: 2. Of those that a mesh axis runs over, the one named last changes fastest.
Arguments:
- data: bfloat16 [64, 256, 16384], P('subj', None, 'vert'), may hold values from -6 to 6
- template: bfloat16 [256, 16384], P(None, 'vert'), may hold values from -6 to 6
- centres: int32 [128], P('vert'), may hold values from 0 to 16383, as said below
- neighbours: int32 [128, 128], P('vert'), may hold values from -128 to 127, as said below
Outputs:
- aligned: bfloat16 [64, 256, 16384], P('subj', None, 'vert')
- new_template: float32 [256, 16384], P(None, 'vert')
The draws below stay inside these ranges and needn't reach their ends.
Inputs may be any that keep to these rules, and one draw needn't show every extreme that they name: The 16 centres of each aligned block of 16 entries are distinct vertices of the matching block of 2048 vertices, and include that block's first and last vertex. `neighbours`: A searchlight's 128 offsets are distinct and include -128 and 127.
All inputs are finite; a program needn't handle non-finite values.
Results may differ from the reference program's by a relative error of at most 0.0005.
Values may be sent and summed in bfloat16 or wider, within the bound.
A program may use at most 64 MiB of HBM per device.

```python
import jax
import jax.numpy as jnp
from jax import lax

K = 128
TF = 256
NS_STEPS = 4
VD = 2048
CEN_DEV = 16
SUBJECTS = 64
VERTS = 16384
CENTRES = 128


def draw_centres(key, part):
    blocks = CENTRES // CEN_DEV
    keys = jax.random.split(key, blocks)

    def one_block(block_key, index):
        inner = jax.random.permutation(block_key, VD - 2)[:CEN_DEV - 2] + 1
        ends = jnp.array([0, VD - 1], jnp.int32)
        return jnp.concatenate([ends, inner.astype(jnp.int32)]) + index * VD
    return jax.vmap(one_block)(keys, jnp.arange(blocks, dtype=jnp.int32)).reshape(-1).astype(jnp.int32)


def draw_neighbours(key, part):
    keys = jax.random.split(jax.random.fold_in(key, 7), CENTRES)

    def one_light(light_key):
        inner = jax.random.permutation(light_key, 2 * K - 2)[:K - 2] + 1 - K
        ends = jnp.array([-K, K - 1], jnp.int32)
        return jnp.concatenate([ends, inner.astype(jnp.int32)])
    return jax.vmap(one_light)(keys).astype(jnp.int32)


def level_of(rng, shape, cuts, smallest, high):
    def one(axis_at, blocks):
        heights = jax.random.uniform(jax.random.fold_in(jax.random.fold_in(rng, 6), axis_at), (blocks,), jnp.float32, smallest / len(cuts), high / len(cuts))
        return jnp.repeat(jnp.exp(heights), shape[axis_at] // blocks).reshape((-1,) + (1,) * (len(shape) - axis_at - 1))

    gain = one(*cuts[0])
    for cut in cuts[1:]:
        gain = gain * one(*cut)
    return gain


def gaussian(stream_key, dims, scale, limit, pieces=(), kind=jnp.bfloat16):
    result = jax.random.normal(stream_key, dims, jnp.float32) * scale
    if len(pieces) > 0:
        result = level_of(stream_key, dims, pieces, -0.22, 0.18) * result
    return jnp.clip(result, min=-limit, max=limit).astype(kind)


def setup_inputs(seed: int = 0) -> dict:
    arg_keys = jax.random.split(jax.random.key(seed), 5)
    data = gaussian(arg_keys[0], (SUBJECTS, TF, VERTS), 1.0, 6.0, ((0, 32), (2, 8)))
    template = gaussian(arg_keys[1], (TF, VERTS), 1.0, 6.0, ((1, 8),))
    centres = draw_centres(jax.random.fold_in(arg_keys[4], 71), 0)
    neighbours = draw_neighbours(jax.random.fold_in(arg_keys[4], 71), 0)
    return dict(data=data, template=template, centres=centres, neighbours=neighbours)


def polar_factor(cross_cov):
    norm_sq = lax.optimization_barrier(jnp.sum(cross_cov * cross_cov, axis=(-2, -1), keepdims=True))
    factor = cross_cov / jnp.sqrt(norm_sq + 1e-06)
    for sweep in range(NS_STEPS):
        gram_mat = jnp.einsum('...kj,...ki->...ji', factor, factor, precision=lax.Precision.HIGHEST)
        factor = 1.5 * factor - 0.5 * jnp.einsum('...kj,...ji->...ki', factor, gram_mat, precision=lax.Precision.HIGHEST)
    return factor

def reference(data, template, centres, neighbours):
    halo_width = neighbours.shape[1]
    n_verts = data.shape[2]
    n_frames = data.shape[1]
    places = centres[:, None] + halo_width + neighbours
    flat_pos = places.reshape(-1).astype(jnp.int32)
    hit_counts = jnp.zeros((n_verts + 2 * halo_width,), jnp.float32).at[flat_pos].add(1.0)
    divisor = jnp.maximum(hit_counts[halo_width:halo_width + n_verts], 1.0)
    padded_template = jnp.pad(template, ((0, 0), (halo_width, halo_width)))
    template_cols = padded_template[:, flat_pos].reshape(n_frames, -1, halo_width).astype(jnp.float32)

    def one_subject(carry, frames):
        padded = jnp.pad(frames, ((0, 0), (halo_width, halo_width)))
        picked = padded[:, flat_pos].reshape(n_frames, -1, halo_width).astype(jnp.float32)
        cross_cov = jnp.einsum('tck,tcj->ckj', picked, template_cols, precision=lax.Precision.HIGHEST)
        rotation = polar_factor(cross_cov)
        rotated = jnp.einsum('tck,ckj->tcj', picked, rotation, precision=lax.Precision.HIGHEST)
        summed = jnp.zeros((n_frames, n_verts + 2 * halo_width), jnp.float32).at[:, flat_pos].add(rotated.reshape(n_frames, -1))
        mapped = summed[:, halo_width:halo_width + n_verts] / divisor
        return (carry + mapped, mapped.astype(jnp.bfloat16))
    total, aligned = lax.scan(one_subject, jnp.zeros((n_frames, n_verts), jnp.float32), data)
    return (aligned, total / data.shape[0])
```

```python
import functools

import jax
import jax.numpy as jnp
from jax import lax
from jax.experimental import pallas as pl
from jax.experimental.pallas import tpu as pltpu
from jax.sharding import PartitionSpec as P

NS_STEPS = 4
MESH = pl.DeviceIdType.MESH
ANY = pl.BlockSpec(memory_space=pl.ANY)
VM = pl.BlockSpec(memory_space=pltpu.VMEM)
SM = pl.BlockSpec(memory_space=pltpu.SMEM)
F32, BF16 = jnp.float32, jnp.bfloat16
LANES = 128


def dot(a, b, dims):
    return lax.dot_general(a, b, (dims, ((), ())), preferred_element_type=F32)


NN, NT, TN = ((1,), (0,)), ((1,), (1,)), ((0,), (0,))


def pieces(x):
    hi = x.astype(BF16)
    return hi, (x - hi.astype(F32)).astype(BF16)


def halo_kernel(n, data, tmpl, left_d, right_d, left_t, right_t, ssem, rsem):
    v = lax.axis_index("vert")
    width = left_d.shape[2]
    own = data.shape[2]
    barrier = pltpu.get_barrier_semaphore()
    lower, upper = v > 0, v < n - 1

    def greet(other):
        pl.semaphore_signal(barrier, inc=1, device_id={"vert": other}, device_id_type=MESH)

    pl.when(lower)(lambda: greet(v - 1))
    pl.when(upper)(lambda: greet(v + 1))
    pl.semaphore_wait(barrier, jnp.minimum(v, 1) + jnp.minimum(n - 1 - v, 1))
    last, first = pl.ds(own - width, width), pl.ds(0, width)

    def copies(up):
        cols = last if up else first
        k = 0 if up else 2
        to = {"vert": v + 1 if up else v - 1}
        return [
            pltpu.make_async_remote_copy(
                data.at[:, :, cols], left_d if up else right_d, ssem.at[k], rsem.at[k],
                device_id=to, device_id_type=MESH),
            pltpu.make_async_remote_copy(
                tmpl.at[:, cols], left_t if up else right_t, ssem.at[k + 1], rsem.at[k + 1],
                device_id=to, device_id_type=MESH),
        ]

    def start(up):
        for c in copies(up):
            c.start()

    def sent(up):
        for c in copies(up):
            c.wait_send()

    def received(up):
        for c in copies(up):
            c.wait_recv()

    pl.when(upper)(lambda: start(True))
    pl.when(lower)(lambda: start(False))
    pl.when(upper)(lambda: sent(True))
    pl.when(lower)(lambda: sent(False))
    pl.when(lower)(lambda: received(True))
    pl.when(upper)(lambda: received(False))


def halos(data, template, n, width):
    s, t, _ = data.shape
    hd = jax.ShapeDtypeStruct((s, t, width), data.dtype)
    ht = jax.ShapeDtypeStruct((t, width), template.dtype)
    return pl.pallas_call(
        functools.partial(halo_kernel, n),
        out_shape=(hd, hd, ht, ht),
        in_specs=[ANY, ANY],
        out_specs=(ANY,) * 4,
        scratch_shapes=[pltpu.SemaphoreType.DMA((4,)), pltpu.SemaphoreType.DMA((4,))],
        compiler_params=pltpu.CompilerParams(collective_id=0, has_side_effects=True),
        name="halo",
    )(data, template)


def align_kernel(n, unroll, cen, nb, data, tmpl, left_d, right_d, left_t, right_t,
                 aligned, partial, own_edge, out_edge, hits, wide, acc, sem):
    ns, nt, own = data.shape
    lights, width = nb.shape
    span = 3 * LANES
    tiles = own // LANES
    v = lax.axis_index("vert")

    def rows(i):
        return pl.ds(i * nt, nt)

    mid, lo, hi = pl.ds(width, own), pl.ds(0, width), pl.ds(width + own, width)
    loads = [pltpu.make_async_copy(data.at[i], wide.at[rows(i), mid], sem.at[i]) for i in range(ns)]
    loads.append(pltpu.make_async_copy(tmpl, wide.at[rows(ns), mid], sem.at[ns]))
    for c in loads:
        c.start()

    def side(cols, d, t, k):
        cs = [pltpu.make_async_copy(d.at[i], wide.at[rows(i), cols], sem.at[k + i]) for i in range(ns)]
        return cs + [pltpu.make_async_copy(t, wide.at[rows(ns), cols], sem.at[k + ns])]

    def begin(cols, d, t, k):
        for c in side(cols, d, t, k):
            c.start()

    def end(cols, d, t, k):
        for c in side(cols, d, t, k):
            c.wait()

    def blank(cols):
        wide[:, cols] = jnp.zeros((wide.shape[0], width), wide.dtype)

    left = (lo, left_d, left_t, ns + 1)
    right = (hi, right_d, right_t, 2 * ns + 2)
    pl.when(v > 0)(lambda: begin(*left))
    pl.when(v < n - 1)(lambda: begin(*right))
    pl.when(v == 0)(lambda: blank(lo))
    pl.when(v == n - 1)(lambda: blank(hi))
    acc[...] = jnp.zeros_like(acc)
    for c in loads:
        c.wait()
    pl.when(v > 0)(lambda: end(*left))
    pl.when(v < n - 1)(lambda: end(*right))

    ones = jnp.ones((16, width), BF16)
    none = jnp.zeros((16, width), BF16)

    def group(g, _):
        where, picks, xs, zs = [], [], [], []
        for u in range(unroll):
            c = g * unroll + u
            local = lax.rem(cen[c], own)
            tile = lax.div(local, LANES)
            base = pl.multiple_of(tile * LANES, LANES)
            target = nb[pl.ds(c, 1), :] + (width + local - base)
            pick = (lax.broadcasted_iota(jnp.int32, (span, width), 0) == target)
            pick = pick.astype(F32).astype(BF16)
            got = dot(wide[:, pl.ds(base, span)], pick, NN).astype(BF16)
            x = [got[i * nt:(i + 1) * nt] for i in range(ns)]
            m = got[ns * nt:]
            z = dot(m, jnp.concatenate(x, axis=1), TN)
            where.append(base)
            picks.append(pick)
            xs.append(x)
            for i in range(ns):
                zi = z[:, i * width:(i + 1) * width]
                norm = jnp.sum(zi * zi, axis=(0, 1), keepdims=True)
                zs.append(zi * (1.0 / jnp.sqrt(norm + 1e-06)))
        for step in range(NS_STEPS):
            grams = []
            for z in zs:
                zh, zl = pieces(z)
                a = jnp.concatenate([zh, zl], axis=1)
                b = jnp.concatenate(
                    [jnp.concatenate([zh, zh], axis=1), jnp.concatenate([zl, zl], axis=1)], axis=0)
                p = dot(a, b, NT)
                grams.append((p[:, :width] + p[:, width:], zh, zl))
            nxt = []
            for z, (gram, zh, zl) in zip(zs, grams):
                gh, gl = pieces(gram)
                a = jnp.concatenate([gh, gl], axis=1)
                b = jnp.concatenate([zh, zl], axis=1)
                p = dot(a, jnp.concatenate([b, b], axis=0), NN)
                nxt.append(1.5 * z - 0.5 * (p[:, :width] + p[:, width:]))
            zs = nxt
        for u in range(unroll):
            parts = []
            for i in range(ns):
                zh, zl = pieces(zs[u * ns + i])
                x = xs[u][i]
                turned = dot(jnp.concatenate([x, x], axis=1), jnp.concatenate([zh, zl], axis=1), NT)
                parts.append(jnp.concatenate(pieces(turned), axis=1))
            parts.append(jnp.concatenate([ones, none], axis=1))
            spread = dot(
                jnp.concatenate(parts, axis=0),
                jnp.concatenate([picks[u], picks[u]], axis=1), NT)
            acc[:, pl.ds(where[u], span)] += spread
        return 0

    lax.fori_loop(0, lights // unroll, group, 0)
    hits[...] = acc[ns * nt:ns * nt + 8, :]
    for i in range(ns):
        own_edge[0, i] = acc[rows(i), pl.ds(width, width)]
        own_edge[1, i] = acc[rows(i), pl.ds(own, width)]
        out_edge[0, i] = acc[rows(i), lo]
        out_edge[1, i] = acc[rows(i), hi]
    for t in range(1, tiles - 1):
        src = pl.ds((t + 1) * LANES, LANES)
        dst = pl.ds(t * LANES, LANES)
        inv = 1.0 / jnp.maximum(acc[pl.ds(ns * nt, 1), src], 1.0)
        total = None
        for i in range(ns):
            mapped = acc[rows(i), src] * inv
            aligned[i, :, dst] = mapped.astype(BF16)
            total = mapped if total is None else total + mapped
        partial[:, dst] = total


def align(centres, neighbours, data, template, sides, n):
    ns, nt, own = data.shape
    lights, width = neighbours.shape
    wide = own + 2 * width
    edge = jax.ShapeDtypeStruct((2, ns, nt, width), F32)
    return pl.pallas_call(
        functools.partial(align_kernel, n, 4),
        out_shape=(
            jax.ShapeDtypeStruct(data.shape, BF16),
            jax.ShapeDtypeStruct((nt, own), F32),
            edge, edge,
            jax.ShapeDtypeStruct((8, wide), F32),
        ),
        in_specs=[SM, VM] + [ANY] * 6,
        out_specs=(VM,) * 5,
        scratch_shapes=[
            pltpu.VMEM(((ns + 1) * nt, wide), BF16),
            pltpu.VMEM((ns * nt + 16, wide), F32),
            pltpu.SemaphoreType.DMA((3 * (ns + 1),)),
        ],
        compiler_params=pltpu.CompilerParams(vmem_limit_bytes=56 << 20),
        name="align",
    )(centres, neighbours, data, template, *sides)


def passed_along(array, axis, by):
    size = lax.axis_size(axis)
    pairs = [(i, i + by) for i in range(size) if 0 <= i + by < size]
    return lax.ppermute(array, axis, pairs)


def local(n, data, template, centres, neighbours):
    width = neighbours.shape[1]
    own = data.shape[2]
    sides = halos(data, template, n, width)
    aligned, partial, own_edge, out_edge, hits = align(centres, neighbours, data, template, sides, n)
    from_upper = passed_along((out_edge[0], hits[0, :width]), "vert", -1)
    from_lower = passed_along((out_edge[1], hits[0, own + width:]), "vert", 1)
    lo_hits = jnp.maximum(hits[0, width:2 * width] + from_lower[1], 1.0)
    hi_hits = jnp.maximum(hits[0, own:own + width] + from_upper[1], 1.0)
    lo = (own_edge[0] + from_lower[0]) / lo_hits
    hi = (own_edge[1] + from_upper[0]) / hi_hits
    aligned = lax.dynamic_update_slice(aligned, lo.astype(BF16), (0, 0, 0))
    aligned = lax.dynamic_update_slice(aligned, hi.astype(BF16), (0, 0, own - width))
    partial = lax.dynamic_update_slice(partial, jnp.sum(lo, axis=0), (0, 0))
    partial = lax.dynamic_update_slice(partial, jnp.sum(hi, axis=0), (0, own - width))
    total = lax.psum(partial, "subj")
    return aligned, total / (data.shape[0] * lax.axis_size("subj"))


def solution(mesh):
    in_specs = (P("subj", None, "vert"), P(None, "vert"), P("vert"), P("vert", None))
    out_specs = (P("subj", None, "vert"), P(None, "vert"))
    return jax.shard_map(
        functools.partial(local, mesh.shape["vert"]), mesh=mesh,
        in_specs=in_specs, out_specs=out_specs, check_vma=False)
```

```python
import functools

import jax
import jax.numpy as jnp
from jax import lax
from jax.experimental import pallas as pl
from jax.experimental.pallas import tpu as pltpu
from jax.sharding import PartitionSpec as P

NS_STEPS = 4
MESH = pl.DeviceIdType.MESH
ANY = pl.BlockSpec(memory_space=pl.ANY)
VM = pl.BlockSpec(memory_space=pltpu.VMEM)
SM = pl.BlockSpec(memory_space=pltpu.SMEM)
F32, BF16 = jnp.float32, jnp.bfloat16
LANES = 128


def dot(a, b, dims):
    return lax.dot_general(a, b, (dims, ((), ())), preferred_element_type=F32)


NN, NT, TN = ((1,), (0,)), ((1,), (1,)), ((0,), (0,))


def pieces(x):
    hi = x.astype(BF16)
    return hi, (x - hi.astype(F32)).astype(BF16)


def halo_kernel(n, data, tmpl, left_d, right_d, left_t, right_t, ssem, rsem):
    v = lax.axis_index("vert")
    width = left_d.shape[2]
    own = data.shape[2]
    barrier = pltpu.get_barrier_semaphore()
    lower, upper = v > 0, v < n - 1

    def greet(other):
        pl.semaphore_signal(barrier, inc=1, device_id={"vert": other}, device_id_type=MESH)

    pl.when(lower)(lambda: greet(v - 1))
    pl.when(upper)(lambda: greet(v + 1))
    pl.semaphore_wait(barrier, jnp.minimum(v, 1) + jnp.minimum(n - 1 - v, 1))
    last, first = pl.ds(own - width, width), pl.ds(0, width)

    def copies(up):
        cols = last if up else first
        k = 0 if up else 2
        to = {"vert": v + 1 if up else v - 1}
        return [
            pltpu.make_async_remote_copy(
                data.at[:, :, cols], left_d if up else right_d, ssem.at[k], rsem.at[k],
                device_id=to, device_id_type=MESH),
            pltpu.make_async_remote_copy(
                tmpl.at[:, cols], left_t if up else right_t, ssem.at[k + 1], rsem.at[k + 1],
                device_id=to, device_id_type=MESH),
        ]

    def start(up):
        for c in copies(up):
            c.start()

    def sent(up):
        for c in copies(up):
            c.wait_send()

    def received(up):
        for c in copies(up):
            c.wait_recv()

    pl.when(upper)(lambda: start(True))
    pl.when(lower)(lambda: start(False))
    pl.when(upper)(lambda: sent(True))
    pl.when(lower)(lambda: sent(False))
    pl.when(lower)(lambda: received(True))
    pl.when(upper)(lambda: received(False))


def halos(data, template, n, width):
    s, t, _ = data.shape
    hd = jax.ShapeDtypeStruct((s, t, width), data.dtype)
    ht = jax.ShapeDtypeStruct((t, width), template.dtype)
    return pl.pallas_call(
        functools.partial(halo_kernel, n),
        out_shape=(hd, hd, ht, ht),
        in_specs=[ANY, ANY],
        out_specs=(ANY,) * 4,
        scratch_shapes=[pltpu.SemaphoreType.DMA((4,)), pltpu.SemaphoreType.DMA((4,))],
        compiler_params=pltpu.CompilerParams(collective_id=0, has_side_effects=True),
        name="halo",
    )(data, template)


def align_kernel(n, unroll, cen, nb, data, tmpl, left_d, right_d, left_t, right_t,
                 aligned, partial, own_edge, out_edge, hits, wide, acc, sem):
    ns, nt, own = data.shape
    lights, width = nb.shape
    span = 3 * LANES
    tiles = own // LANES
    v = lax.axis_index("vert")

    def rows(i):
        return pl.ds(i * nt, nt)

    mid, lo, hi = pl.ds(width, own), pl.ds(0, width), pl.ds(width + own, width)
    loads = [pltpu.make_async_copy(data.at[i], wide.at[rows(i), mid], sem.at[i]) for i in range(ns)]
    loads.append(pltpu.make_async_copy(tmpl, wide.at[rows(ns), mid], sem.at[ns]))
    for c in loads:
        c.start()

    def side(cols, d, t, k):
        cs = [pltpu.make_async_copy(d.at[i], wide.at[rows(i), cols], sem.at[k + i]) for i in range(ns)]
        return cs + [pltpu.make_async_copy(t, wide.at[rows(ns), cols], sem.at[k + ns])]

    def begin(cols, d, t, k):
        for c in side(cols, d, t, k):
            c.start()

    def end(cols, d, t, k):
        for c in side(cols, d, t, k):
            c.wait()

    def blank(cols):
        wide[:, cols] = jnp.zeros((wide.shape[0], width), wide.dtype)

    left = (lo, left_d, left_t, ns + 1)
    right = (hi, right_d, right_t, 2 * ns + 2)
    pl.when(v > 0)(lambda: begin(*left))
    pl.when(v < n - 1)(lambda: begin(*right))
    pl.when(v == 0)(lambda: blank(lo))
    pl.when(v == n - 1)(lambda: blank(hi))
    acc[...] = jnp.zeros_like(acc)
    for c in loads:
        c.wait()
    pl.when(v > 0)(lambda: end(*left))
    pl.when(v < n - 1)(lambda: end(*right))

    ones = jnp.ones((16, width), BF16)
    none = jnp.zeros((16, width), BF16)

    def group(g, _):
        where, picks, xs, zs = [], [], [], []
        for u in range(unroll):
            c = g * unroll + u
            local = lax.rem(cen[c], own)
            tile = lax.div(local, LANES)
            base = pl.multiple_of(tile * LANES, LANES)
            target = nb[pl.ds(c, 1), :] + (width + local - base)
            pick = (lax.broadcasted_iota(jnp.int32, (span, width), 0) == target)
            pick = pick.astype(F32).astype(BF16)
            got = dot(wide[:, pl.ds(base, span)], pick, NN).astype(BF16)
            x = [got[i * nt:(i + 1) * nt] for i in range(ns)]
            m = got[ns * nt:]
            z = dot(m, jnp.concatenate(x, axis=1), TN)
            where.append(base)
            picks.append(pick)
            xs.append(x)
            for i in range(ns):
                zi = z[:, i * width:(i + 1) * width]
                norm = jnp.sum(zi * zi, axis=(0, 1), keepdims=True)
                zs.append(zi * (1.0 / jnp.sqrt(norm + 1e-06)))
        for step in range(NS_STEPS):
            grams = []
            for z in zs:
                zh, zl = pieces(z)
                a = jnp.concatenate([zh, zl], axis=1)
                b = jnp.concatenate(
                    [jnp.concatenate([zh, zh], axis=1), jnp.concatenate([zl, zl], axis=1)], axis=0)
                p = dot(a, b, NT)
                grams.append((p[:, :width] + p[:, width:], zh, zl))
            nxt = []
            for z, (gram, zh, zl) in zip(zs, grams):
                gh, gl = pieces(gram)
                a = jnp.concatenate([gh, gl], axis=1)
                b = jnp.concatenate([zh, zl], axis=1)
                p = dot(a, jnp.concatenate([b, b], axis=0), NN)
                nxt.append(1.5 * z - 0.5 * (p[:, :width] + p[:, width:]))
            zs = nxt
        for u in range(unroll):
            parts = []
            for i in range(ns):
                zh, zl = pieces(zs[u * ns + i])
                x = xs[u][i]
                turned = dot(jnp.concatenate([x, x], axis=1), jnp.concatenate([zh, zl], axis=1), NT)
                parts.append(jnp.concatenate(pieces(turned), axis=1))
            parts.append(jnp.concatenate([ones, none], axis=1))
            spread = dot(
                jnp.concatenate(parts, axis=0),
                jnp.concatenate([picks[u], picks[u]], axis=1), NT)
            acc[:, pl.ds(where[u], span)] += spread
        return 0

    lax.fori_loop(0, lights // unroll, group, 0)
    hits[...] = acc[ns * nt:ns * nt + 8, :]
    for i in range(ns):
        own_edge[0, i] = acc[rows(i), pl.ds(width, width)]
        own_edge[1, i] = acc[rows(i), pl.ds(own, width)]
        out_edge[0, i] = acc[rows(i), lo]
        out_edge[1, i] = acc[rows(i), hi]
    for t in range(1, tiles - 1):
        src = pl.ds((t + 1) * LANES, LANES)
        dst = pl.ds(t * LANES, LANES)
        inv = 1.0 / jnp.maximum(acc[pl.ds(ns * nt, 1), src], 1.0)
        total = None
        for i in range(ns):
            mapped = acc[rows(i), src] * inv
            aligned[i, :, dst] = mapped.astype(BF16)
            total = mapped if total is None else total + mapped
        partial[:, pl.ds((t - 1) * LANES, LANES)] = total


def align(centres, neighbours, data, template, sides, n):
    ns, nt, own = data.shape
    lights, width = neighbours.shape
    wide = own + 2 * width
    edge = jax.ShapeDtypeStruct((2, ns, nt, width), F32)
    return pl.pallas_call(
        functools.partial(align_kernel, n, 4),
        out_shape=(
            jax.ShapeDtypeStruct(data.shape, BF16),
            jax.ShapeDtypeStruct((nt, own), F32),
            edge, edge,
            jax.ShapeDtypeStruct((8, wide), F32),
        ),
        in_specs=[SM, VM] + [ANY] * 6,
        out_specs=(VM,) * 5,
        scratch_shapes=[
            pltpu.VMEM(((ns + 1) * nt, wide), BF16),
            pltpu.VMEM((ns * nt + 16, wide), F32),
            pltpu.SemaphoreType.DMA((3 * (ns + 1),)),
        ],
        compiler_params=pltpu.CompilerParams(vmem_limit_bytes=56 << 20),
        name="align",
    )(centres, neighbours, data, template, *sides)


NZ, NX, NY = 2, 4, 4
RS, AG = 6, 4
SENDS = 2 * RS + 1 + 2 * AG


def reduce_kernel(n, chunks, part, own_edge, out_edge, hits, out, edge_aligned,
                  full, edge_part, edge_in, hits_in, r1, r2, t1, q1, s1, s2, u1, q2, zin,
                  ssem, rsem, esem, osem):
    s, v = lax.axis_index("subj"), lax.axis_index("vert")
    ns, nt, width = own_edge.shape[1:]
    own = full.shape[1]
    y, x, zh = lax.rem(s, NY), lax.rem(lax.div(s, NY), NX), lax.div(s, NX * NY)

    def place(zh, x, y):
        return {"subj": (zh * NX + x) * NY + y}

    def along(axis, by):
        if axis == 0:
            return place(zh, lax.rem(x + by + NX, NX), y)
        return place(zh, x, lax.rem(y + by + NY, NY))

    across = place(NZ - 1 - zh, x, y)
    barrier = pltpu.get_barrier_semaphore()
    lower, upper = v > 0, v < n - 1

    def greet(to):
        pl.semaphore_signal(barrier, inc=1, device_id=to, device_id_type=MESH)

    for to in (along(0, 1), along(0, -1), along(1, 1), along(1, -1), across):
        greet(to)
    pl.when(lower)(lambda: greet({"vert": v - 1}))
    pl.when(upper)(lambda: greet({"vert": v + 1}))
    pl.semaphore_wait(barrier, 5 + jnp.minimum(v, 1) + jnp.minimum(n - 1 - v, 1))

    def edge_copies(up):
        k = 1 if up else 0
        to = {"vert": v + 1 if up else v - 1}
        cols = pl.ds(width + own, width) if up else pl.ds(0, width)
        return [
            pltpu.make_async_remote_copy(
                out_edge.at[k], edge_in.at[k], esem.at[0, k], esem.at[1, k],
                device_id=to, device_id_type=MESH),
            pltpu.make_async_remote_copy(
                hits.at[:, cols], hits_in.at[k], esem.at[0, 2 + k], esem.at[1, 2 + k],
                device_id=to, device_id_type=MESH),
        ]

    def edge_start(up):
        for c in edge_copies(up):
            c.start()

    def edge_sent(up):
        for c in edge_copies(up):
            c.wait_send()

    def edge_got(up):
        for c in edge_copies(up):
            c.wait_recv()

    def edge_blank(up):
        k = 1 if up else 0
        edge_in[k] = jnp.zeros(edge_in.shape[1:], F32)
        hits_in[k] = jnp.zeros(hits_in.shape[1:], F32)

    pl.when(upper)(lambda: edge_start(True))
    pl.when(lower)(lambda: edge_start(False))
    pl.when(jnp.logical_not(lower))(lambda: edge_blank(True))
    pl.when(jnp.logical_not(upper))(lambda: edge_blank(False))

    def edges():
        pl.when(lower)(lambda: edge_got(True))
        pl.when(upper)(lambda: edge_got(False))
        for side in range(2):
            k = 1 - side
            at = pl.ds(width if side == 0 else own, width)
            inv = 1.0 / jnp.maximum(hits[pl.ds(0, 1), at] + hits_in[k, pl.ds(0, 1), :], 1.0)
            total = None
            for i in range(ns):
                mapped = (own_edge[side, i] + edge_in[k, i]) * inv
                edge_aligned[side, i] = mapped.astype(BF16)
                total = mapped if total is None else total + mapped
            edge_part[:, side * width:(side + 1) * width] = total

    sends = []

    def rs_stages(c, first, axis, p, src, cols, half, r1, r2, t, dst):
        right, left = along(axis, 1), along(axis, -1)

        def go(k, a, b, to):
            d = pltpu.make_async_remote_copy(
                a, b, ssem.at[c, first + k], rsem.at[c, first + k],
                device_id=to, device_id_type=MESH)
            d.start()
            sends.append(d)

        def got(k, b):
            pltpu.make_async_remote_copy(
                b, b, ssem.at[c, first + k], rsem.at[c, first + k],
                device_id=right, device_id_type=MESH).wait_recv()

        def slot(ref, k):
            return ref.at[pl.ds(k * half, half), cols]

        def val(ref, k):
            return ref[pl.ds(k * half, half), cols]

        nxt, far, prv = lax.rem(p + 1, 4), lax.rem(p + 2, 4), lax.rem(p + 3, 4)

        def at(q, h):
            ref, rows, cc = src(q, h)
            return ref.at[rows, cc]

        def load(q, h):
            ref, rows, cc = src(q, h)
            return ref[rows, cc]

        def a():
            go(0, at(far, 0), slot(r1, 0), right)
            go(1, at(far, 1), slot(r1, 1), left)
            go(2, at(nxt, 1), slot(r2, 1), right)
            go(3, at(prv, 0), slot(r2, 2), left)

        def b():
            got(0, slot(r1, 0))
            t[pl.ds(0, half), cols] = load(nxt, 0) + val(r1, 0)
            go(4, slot(t, 0), slot(r2, 0), right)
            got(1, slot(r1, 1))
            t[pl.ds(half, half), cols] = load(prv, 1) + val(r1, 1)
            go(5, slot(t, 1), slot(r2, 3), left)

        def c_():
            got(3, slot(r2, 2))
            got(4, slot(r2, 0))
            dst[pl.ds(0, half), cols] = load(p, 0) + (val(r2, 0) + val(r2, 2))
            got(2, slot(r2, 1))
            got(5, slot(r2, 3))
            dst[pl.ds(half, half), cols] = load(p, 1) + (val(r2, 1) + val(r2, 3))

        return a, b, c_

    def ag_stages(c, first, axis, p, piece):
        right, left = along(axis, 1), along(axis, -1)
        nxt, far, prv = lax.rem(p + 1, 4), lax.rem(p + 2, 4), lax.rem(p + 3, 4)

        def desc(k, ref, to):
            return pltpu.make_async_remote_copy(
                ref, ref, ssem.at[c, first + k], rsem.at[c, first + k],
                device_id=to, device_id_type=MESH)

        def go(k, ref, to):
            d = desc(k, ref, to)
            d.start()
            sends.append(d)

        def a():
            go(0, piece(p, None), right)
            go(1, piece(p, None), left)

        def b():
            desc(0, piece(prv, None), right).wait_recv()
            go(2, piece(prv, 0), right)
            desc(1, piece(nxt, None), right).wait_recv()
            go(3, piece(nxt, 1), left)

        def c_():
            desc(2, piece(far, 0), right).wait_recv()
            desc(3, piece(far, 1), right).wait_recv()

        return a, b, c_

    big, mid, small = nt // 4, nt // 16, nt // 32

    def chunk(c, col, size, order):
        edge = order is None
        first = 1 if edge else order
        second = 1 - first
        pos = (x, y)
        p1, p2 = pos[first], pos[second]
        cols = pl.ds(col, size)

        def rows(q, h, unit, base=0):
            start = base + q * unit
            if h is None:
                return pl.ds(pl.multiple_of(start, unit), unit)
            return pl.ds(pl.multiple_of(start + h * (unit // 2), unit // 2), unit // 2)

        def src1(q, h):
            if edge:
                return edge_part, rows(q, h, big), pl.ds(0, size)
            return part, rows(q, h, big), cols

        def src2(q, h):
            return q1, rows(q, h, mid), cols

        a1, b1, c1 = rs_stages(c, 0, first, p1, src1, cols, big // 2, r1, r2, t1, q1)
        a2, b2, c2 = rs_stages(c, RS, second, p2, src2, cols, mid // 2, s1, s2, u1, q2)
        base = p1 * big

        def piece2(q, h):
            return full.at[rows(q, h, mid, base), cols]

        def piece1(q, h):
            return full.at[rows(q, h, big), cols]

        g2, h2, i2 = ag_stages(c, 2 * RS + 1, second, p2, piece2)
        g1, h1, i1 = ag_stages(c, 2 * RS + 1 + AG, first, p1, piece1)
        kz = 2 * RS
        swap = pltpu.make_async_remote_copy(
            q2.at[:, cols], zin.at[:, cols], ssem.at[c, kz], rsem.at[c, kz],
            device_id=across, device_id_type=MESH)

        def stage0():
            if edge:
                edges()
            a1()

        def stage2():
            c1()
            a2()

        def stage4():
            c2()
            swap.start()
            sends.append(swap)

        def stage5():
            swap.wait_recv()
            mine = pl.ds(pl.multiple_of(base + p2 * mid, mid), mid)
            full[mine, cols] = (q2[:, cols] + zin[:, cols]) * (1.0 / (ns * NZ * NX * NY))
            g2()

        def stage7():
            i2()
            g1()

        def stage9():
            i1()
            if edge:
                half = size // 2
                dst = [(col, 0, half), (col + half, own - half, half)]
            else:
                dst = [(col, col + width, size)]
            for k, (a, b, w) in enumerate(dst):
                d = pltpu.make_async_copy(
                    full.at[:, pl.ds(a, w)], out.at[:, pl.ds(b, w)], osem.at[c + k])
                d.start()
                outs.append(d)

        return stage0, b1, stage2, b2, stage4, stage5, h2, stage7, h1, stage9

    outs = []
    work = [chunk(c, *spec) for c, spec in enumerate(chunks)]
    depth = len(work[0])
    pairs = len(work) // 2
    for wave in range(pairs + depth - 1):
        for k in range(pairs):
            if 0 <= wave - k < depth:
                work[2 * k][wave - k]()
                work[2 * k + 1][wave - k]()
    for d in sends:
        d.wait_send()
    pl.when(upper)(lambda: edge_sent(True))
    pl.when(lower)(lambda: edge_sent(False))
    for d in outs:
        d.wait()


def reduce(partial, own_edge, out_edge, hits, n):
    nt, own = partial.shape
    _, ns, _, width = own_edge.shape
    pairs = 4
    size = own // (2 * pairs)
    chunks = tuple((k * size, size, k % 2) for k in range(2 * pairs - 1))
    chunks += (((2 * pairs - 1) * size, size, None),)

    def rows(k):
        return pltpu.VMEM((k, own), F32)

    sem = pltpu.SemaphoreType.DMA
    return pl.pallas_call(
        functools.partial(reduce_kernel, n, chunks),
        out_shape=(
            jax.ShapeDtypeStruct((nt, own), F32),
            jax.ShapeDtypeStruct((2, ns, nt, width), BF16),
        ),
        in_specs=[VM] * 4,
        out_specs=(ANY, VM),
        scratch_shapes=[
            rows(nt),
            pltpu.VMEM((nt, size), F32),
            pltpu.VMEM((2, ns, nt, width), F32),
            pltpu.VMEM((2, 8, width), F32),
            rows(nt // 4), rows(nt // 2), rows(nt // 4), rows(nt // 4),
            rows(nt // 16), rows(nt // 8), rows(nt // 16), rows(nt // 16), rows(nt // 16),
            sem((2 * pairs, SENDS)), sem((2 * pairs, SENDS)), sem((2, 4)), sem((2 * pairs + 1,)),
        ],
        compiler_params=pltpu.CompilerParams(
            collective_id=1, has_side_effects=True, vmem_limit_bytes=56 << 20),
        name="reduce",
    )(partial, own_edge, out_edge, hits)


def local(n, data, template, centres, neighbours):
    width = neighbours.shape[1]
    own = data.shape[2]
    sides = halos(data, template, n, width)
    aligned, partial, own_edge, out_edge, hits = align(centres, neighbours, data, template, sides, n)
    new_template, edge_aligned = reduce(partial, own_edge, out_edge, hits, n)
    aligned = lax.dynamic_update_slice(aligned, edge_aligned[0], (0, 0, 0))
    aligned = lax.dynamic_update_slice(aligned, edge_aligned[1], (0, 0, own - width))
    return aligned, new_template


def solution(mesh):
    in_specs = (P("subj", None, "vert"), P(None, "vert"), P("vert"), P("vert", None))
    out_specs = (P("subj", None, "vert"), P(None, "vert"))
    return jax.shard_map(
        functools.partial(local, mesh.shape["vert"]), mesh=mesh,
        in_specs=in_specs, out_specs=out_specs, check_vma=False)
```

```python
import functools

import jax
import jax.numpy as jnp
from jax import lax
from jax.experimental import pallas as pl
from jax.experimental.pallas import tpu as pltpu
from jax.sharding import PartitionSpec as P

NS_STEPS = 4
MESH = pl.DeviceIdType.MESH
ANY = pl.BlockSpec(memory_space=pl.ANY)
VM = pl.BlockSpec(memory_space=pltpu.VMEM)
HBM = pl.BlockSpec(memory_space=pltpu.HBM)
SM = pl.BlockSpec(memory_space=pltpu.SMEM)
F32, BF16 = jnp.float32, jnp.bfloat16
LANES = 128


def dot(a, b, dims):
    return lax.dot_general(a, b, (dims, ((), ())), preferred_element_type=F32)


NN, NT, TN = ((1,), (0,)), ((1,), (1,)), ((0,), (0,))


def pieces(x):
    hi = x.astype(BF16)
    return hi, (x - hi.astype(F32)).astype(BF16)


def halo_kernel(n, data, tmpl, wide, lsem, ssem, rsem):
    v = lax.axis_index("vert")
    ns, nt, own = data.shape
    width = (wide.shape[1] - own) // 2
    barrier = pltpu.get_barrier_semaphore()
    lower, upper = v > 0, v < n - 1

    def greet(other):
        pl.semaphore_signal(barrier, inc=1, device_id={"vert": other}, device_id_type=MESH)

    def rows(i):
        return pl.ds(i * nt, nt)

    def src(i, cols):
        return data.at[i, :, cols] if i < ns else tmpl.at[:, cols]

    pl.when(lower)(lambda: greet(v - 1))
    pl.when(upper)(lambda: greet(v + 1))
    mine = [
        pltpu.make_async_copy(
            src(i, pl.ds(0, own)), wide.at[rows(i), pl.ds(width, own)], lsem.at[i])
        for i in range(ns + 1)
    ]
    for c in mine:
        c.start()
    pl.semaphore_wait(barrier, jnp.minimum(v, 1) + jnp.minimum(n - 1 - v, 1))

    def copies(up):
        cols = pl.ds(own - width, width) if up else pl.ds(0, width)
        dst = pl.ds(0, width) if up else pl.ds(width + own, width)
        to = {"vert": v + 1 if up else v - 1}
        k = 0 if up else ns + 1
        return [
            pltpu.make_async_remote_copy(
                src(i, cols), wide.at[rows(i), dst], ssem.at[k + i], rsem.at[k + i],
                device_id=to, device_id_type=MESH)
            for i in range(ns + 1)
        ]

    def start(up):
        for c in copies(up):
            c.start()

    def sent(up):
        for c in copies(up):
            c.wait_send()

    def received(up):
        for c in copies(up):
            c.wait_recv()

    def blank(at):
        wide[:, pl.ds(at, width)] = jnp.zeros((wide.shape[0], width), wide.dtype)

    pl.when(upper)(lambda: start(True))
    pl.when(lower)(lambda: start(False))
    pl.when(jnp.logical_not(lower))(lambda: blank(0))
    pl.when(jnp.logical_not(upper))(lambda: blank(width + own))
    for c in mine:
        c.wait()
    pl.when(upper)(lambda: sent(True))
    pl.when(lower)(lambda: sent(False))
    pl.when(lower)(lambda: received(True))
    pl.when(upper)(lambda: received(False))


def halos(data, template, n, width):
    ns, nt, own = data.shape
    sem = pltpu.SemaphoreType.DMA
    return pl.pallas_call(
        functools.partial(halo_kernel, n),
        out_shape=jax.ShapeDtypeStruct(((ns + 1) * nt, own + 2 * width), data.dtype),
        in_specs=[HBM, HBM],
        out_specs=VM,
        scratch_shapes=[sem((ns + 1,)), sem((2 * ns + 2,)), sem((2 * ns + 2,))],
        compiler_params=pltpu.CompilerParams(
            collective_id=0, has_side_effects=True, vmem_limit_bytes=8 << 20),
        name="halo",
    )(*(pltpu.with_memory_space_constraint(a, pltpu.HBM) for a in (data, template)))


def align_kernel(ns, unroll, cen, nb, wide, aligned, partial, own_edge, out_edge, hits, acc):
    lights, width = nb.shape
    nt, own = partial.shape
    span = 3 * LANES
    tiles = own // LANES
    lo, hi = pl.ds(0, width), pl.ds(width + own, width)

    def rows(i):
        return pl.ds(i * nt, nt)

    acc[...] = jnp.zeros_like(acc)
    ones = jnp.ones((16, width), BF16)
    none = jnp.zeros((16, width), BF16)

    def group(g, _):
        where, picks, xs, zs = [], [], [], []
        for u in range(unroll):
            c = g * unroll + u
            local = lax.rem(cen[c], own)
            tile = lax.div(local, LANES)
            base = pl.multiple_of(tile * LANES, LANES)
            target = nb[pl.ds(c, 1), :] + (width + local - base)
            pick = (lax.broadcasted_iota(jnp.int32, (span, width), 0) == target)
            pick = pick.astype(F32).astype(BF16)
            got = dot(wide[:, pl.ds(base, span)], pick, NN).astype(BF16)
            x = [got[i * nt:(i + 1) * nt] for i in range(ns)]
            m = got[ns * nt:]
            z = dot(m, jnp.concatenate(x, axis=1), TN)
            where.append(base)
            picks.append(pick)
            xs.append(x)
            for i in range(ns):
                zi = z[:, i * width:(i + 1) * width]
                norm = jnp.sum(zi * zi, axis=(0, 1), keepdims=True)
                zs.append(zi * (1.0 / jnp.sqrt(norm + 1e-06)))
        for step in range(NS_STEPS):
            grams = []
            for z in zs:
                zh, zl = pieces(z)
                a = jnp.concatenate([zh, zl], axis=1)
                b = jnp.concatenate(
                    [jnp.concatenate([zh, zh], axis=1), jnp.concatenate([zl, zl], axis=1)], axis=0)
                p = dot(a, b, NT)
                grams.append((p[:, :width] + p[:, width:], zh, zl))
            nxt = []
            for z, (gram, zh, zl) in zip(zs, grams):
                gh, gl = pieces(gram)
                a = jnp.concatenate([gh, gl], axis=1)
                b = jnp.concatenate([zh, zl], axis=1)
                p = dot(a, jnp.concatenate([b, b], axis=0), NN)
                nxt.append(1.5 * z - 0.5 * (p[:, :width] + p[:, width:]))
            zs = nxt
        for u in range(unroll):
            parts = []
            for i in range(ns):
                zh, zl = pieces(zs[u * ns + i])
                x = xs[u][i]
                turned = dot(jnp.concatenate([x, x], axis=1), jnp.concatenate([zh, zl], axis=1), NT)
                parts.append(jnp.concatenate(pieces(turned), axis=1))
            parts.append(jnp.concatenate([ones, none], axis=1))
            spread = dot(
                jnp.concatenate(parts, axis=0),
                jnp.concatenate([picks[u], picks[u]], axis=1), NT)
            acc[:, pl.ds(where[u], span)] += spread
        return 0

    lax.fori_loop(0, lights // unroll, group, 0)
    hits[...] = acc[ns * nt:ns * nt + 8, :]
    for i in range(ns):
        own_edge[0, i] = acc[rows(i), pl.ds(width, width)]
        own_edge[1, i] = acc[rows(i), pl.ds(own, width)]
        out_edge[0, i] = acc[rows(i), lo]
        out_edge[1, i] = acc[rows(i), hi]
    for t in range(1, tiles - 1):
        src = pl.ds((t + 1) * LANES, LANES)
        dst = pl.ds(t * LANES, LANES)
        inv = 1.0 / jnp.maximum(acc[pl.ds(ns * nt, 1), src], 1.0)
        total = None
        for i in range(ns):
            mapped = acc[rows(i), src] * inv
            aligned[i, :, dst] = mapped.astype(BF16)
            total = mapped if total is None else total + mapped
        partial[:, pl.ds((t - 1) * LANES, LANES)] = total


def align(centres, neighbours, wide, shape):
    ns, nt, own = shape
    width = neighbours.shape[1]
    edge = jax.ShapeDtypeStruct((2, ns, nt, width), F32)
    return pl.pallas_call(
        functools.partial(align_kernel, ns, 4),
        out_shape=(
            jax.ShapeDtypeStruct(shape, BF16),
            jax.ShapeDtypeStruct((nt, own), F32),
            edge, edge,
            jax.ShapeDtypeStruct((8, wide.shape[1]), F32),
        ),
        in_specs=[SM, VM, VM],
        out_specs=(VM,) * 5,
        scratch_shapes=[pltpu.VMEM((ns * nt + 16, wide.shape[1]), F32)],
        compiler_params=pltpu.CompilerParams(vmem_limit_bytes=24 << 20),
        name="align",
    )(centres, neighbours, wide)


NZ, NX, NY = 2, 4, 4
ORDER = (
    0, 1, 2, 3, 4, 5, 16, 17, 8, 9, 18, 19, 10, 11, 6, 7,
    20, 21, 12, 13, 24, 25, 26, 27, 22, 23, 14, 15, 28, 29, 41, 40,
    32, 43, 42, 33, 34, 35, 30, 31, 44, 45, 36, 37, 48, 49, 50, 51,
    46, 47, 38, 39, 52, 53, 54, 55, 56, 57, 72, 64, 58, 73, 65, 59,
    80, 74, 66, 60, 81, 75, 67, 61, 82, 96, 76, 88, 68, 62, 83, 97,
    77, 89, 69, 63, 84, 98, 78, 90, 70, 104, 85, 99, 79, 91, 71, 105,
    86, 100, 92, 106, 87, 101, 93, 107, 102, 94, 108, 103, 95, 109, 110, 111,
)
RS, AG = 6, 4
SENDS = 2 * RS + 1 + 2 * AG


def reduce_kernel(n, chunks, part, own_edge, out_edge, hits, out, edge_aligned,
                  full, edge_part, edge_in, hits_in, r1, r2, t1, q1, s1, s2, u1, q2, zin,
                  ssem, rsem, esem, osem):
    s, v = lax.axis_index("subj"), lax.axis_index("vert")
    ns, nt, width = own_edge.shape[1:]
    own = full.shape[1]
    y, x, zh = lax.rem(s, NY), lax.rem(lax.div(s, NY), NX), lax.div(s, NX * NY)

    def place(zh, x, y):
        return {"subj": (zh * NX + x) * NY + y}

    def along(axis, by):
        if axis == 0:
            return place(zh, lax.rem(x + by + NX, NX), y)
        return place(zh, x, lax.rem(y + by + NY, NY))

    across = place(NZ - 1 - zh, x, y)
    barrier = pltpu.get_barrier_semaphore()
    lower, upper = v > 0, v < n - 1

    def greet(to):
        pl.semaphore_signal(barrier, inc=1, device_id=to, device_id_type=MESH)

    for to in (along(0, 1), along(0, -1), along(1, 1), along(1, -1), across):
        greet(to)
    pl.when(lower)(lambda: greet({"vert": v - 1}))
    pl.when(upper)(lambda: greet({"vert": v + 1}))
    pl.semaphore_wait(barrier, 5 + jnp.minimum(v, 1) + jnp.minimum(n - 1 - v, 1))

    def edge_copies(up):
        k = 1 if up else 0
        to = {"vert": v + 1 if up else v - 1}
        cols = pl.ds(width + own, width) if up else pl.ds(0, width)
        return [
            pltpu.make_async_remote_copy(
                out_edge.at[k], edge_in.at[k], esem.at[0, k], esem.at[1, k],
                device_id=to, device_id_type=MESH),
            pltpu.make_async_remote_copy(
                hits.at[:, cols], hits_in.at[k], esem.at[0, 2 + k], esem.at[1, 2 + k],
                device_id=to, device_id_type=MESH),
        ]

    def edge_start(up):
        for c in edge_copies(up):
            c.start()

    def edge_sent(up):
        for c in edge_copies(up):
            c.wait_send()

    def edge_got(up):
        for c in edge_copies(up):
            c.wait_recv()

    def edge_blank(up):
        k = 1 if up else 0
        edge_in[k] = jnp.zeros(edge_in.shape[1:], F32)
        hits_in[k] = jnp.zeros(hits_in.shape[1:], F32)

    pl.when(upper)(lambda: edge_start(True))
    pl.when(lower)(lambda: edge_start(False))
    pl.when(jnp.logical_not(lower))(lambda: edge_blank(True))
    pl.when(jnp.logical_not(upper))(lambda: edge_blank(False))

    def edges():
        pl.when(lower)(lambda: edge_got(True))
        pl.when(upper)(lambda: edge_got(False))
        for side in range(2):
            k = 1 - side
            at = pl.ds(width if side == 0 else own, width)
            inv = 1.0 / jnp.maximum(hits[pl.ds(0, 1), at] + hits_in[k, pl.ds(0, 1), :], 1.0)
            total = None
            for i in range(ns):
                mapped = (own_edge[side, i] + edge_in[k, i]) * inv
                edge_aligned[side, i] = mapped.astype(BF16)
                total = mapped if total is None else total + mapped
            edge_part[:, side * width:(side + 1) * width] = total

    sends = []

    def rs_stages(c, first, axis, p, src, cols, half, r1, r2, t, dst):
        right, left = along(axis, 1), along(axis, -1)

        def go(k, a, b, to):
            d = pltpu.make_async_remote_copy(
                a, b, ssem.at[c, first + k], rsem.at[c, first + k],
                device_id=to, device_id_type=MESH)
            d.start()
            sends.append(d)

        def got(k, b):
            pltpu.make_async_remote_copy(
                b, b, ssem.at[c, first + k], rsem.at[c, first + k],
                device_id=right, device_id_type=MESH).wait_recv()

        def slot(ref, k):
            return ref.at[pl.ds(k * half, half), cols]

        def val(ref, k):
            return ref[pl.ds(k * half, half), cols]

        nxt, far, prv = lax.rem(p + 1, 4), lax.rem(p + 2, 4), lax.rem(p + 3, 4)

        def at(q, h):
            ref, rows, cc = src(q, h)
            return ref.at[rows, cc]

        def load(q, h):
            ref, rows, cc = src(q, h)
            return ref[rows, cc]

        def a():
            go(0, at(far, 0), slot(r1, 0), right)
            go(1, at(far, 1), slot(r1, 1), left)
            go(2, at(nxt, 1), slot(r2, 1), right)
            go(3, at(prv, 0), slot(r2, 2), left)

        def b_right():
            got(0, slot(r1, 0))
            t[pl.ds(0, half), cols] = load(nxt, 0) + val(r1, 0)
            go(4, slot(t, 0), slot(r2, 0), right)

        def b_left():
            got(1, slot(r1, 1))
            t[pl.ds(half, half), cols] = load(prv, 1) + val(r1, 1)
            go(5, slot(t, 1), slot(r2, 3), left)

        def c_():
            got(3, slot(r2, 2))
            got(4, slot(r2, 0))
            dst[pl.ds(0, half), cols] = load(p, 0) + (val(r2, 0) + val(r2, 2))
            got(2, slot(r2, 1))
            got(5, slot(r2, 3))
            dst[pl.ds(half, half), cols] = load(p, 1) + (val(r2, 1) + val(r2, 3))

        return a, b_right, b_left, c_

    def ag_stages(c, first, axis, p, piece):
        right, left = along(axis, 1), along(axis, -1)
        nxt, far, prv = lax.rem(p + 1, 4), lax.rem(p + 2, 4), lax.rem(p + 3, 4)

        def desc(k, ref, to):
            return pltpu.make_async_remote_copy(
                ref, ref, ssem.at[c, first + k], rsem.at[c, first + k],
                device_id=to, device_id_type=MESH)

        def go(k, ref, to):
            d = desc(k, ref, to)
            d.start()
            sends.append(d)

        def a():
            go(0, piece(p, None), right)
            go(1, piece(p, None), left)

        def b_right():
            desc(0, piece(prv, None), right).wait_recv()
            go(2, piece(prv, 0), right)

        def b_left():
            desc(1, piece(nxt, None), right).wait_recv()
            go(3, piece(nxt, 1), left)

        def c_():
            desc(2, piece(far, 0), right).wait_recv()
            desc(3, piece(far, 1), right).wait_recv()

        return a, b_right, b_left, c_

    big, mid, small = nt // 4, nt // 16, nt // 32

    def chunk(c, col, size, order):
        edge = order is None
        first = 1 if edge else order
        second = 1 - first
        pos = (x, y)
        p1, p2 = pos[first], pos[second]
        cols = pl.ds(col, size)

        def rows(q, h, unit, base=0):
            start = base + q * unit
            if h is None:
                return pl.ds(pl.multiple_of(start, unit), unit)
            return pl.ds(pl.multiple_of(start + h * (unit // 2), unit // 2), unit // 2)

        def src1(q, h):
            if edge:
                return edge_part, rows(q, h, big), pl.ds(0, size)
            return part, rows(q, h, big), cols

        def src2(q, h):
            return q1, rows(q, h, mid), cols

        a1, b1r, b1l, c1 = rs_stages(c, 0, first, p1, src1, cols, big // 2, r1, r2, t1, q1)
        a2, b2r, b2l, c2 = rs_stages(c, RS, second, p2, src2, cols, mid // 2, s1, s2, u1, q2)
        base = p1 * big

        def piece2(q, h):
            return full.at[rows(q, h, mid, base), cols]

        def piece1(q, h):
            return full.at[rows(q, h, big), cols]

        g2, h2r, h2l, i2 = ag_stages(c, 2 * RS + 1, second, p2, piece2)
        g1, h1r, h1l, i1 = ag_stages(c, 2 * RS + 1 + AG, first, p1, piece1)
        kz = 2 * RS
        swap = pltpu.make_async_remote_copy(
            q2.at[:, cols], zin.at[:, cols], ssem.at[c, kz], rsem.at[c, kz],
            device_id=across, device_id_type=MESH)

        def stage0():
            if edge:
                edges()
            a1()

        def stage2():
            c1()
            a2()

        def stage4():
            c2()
            swap.start()
            sends.append(swap)

        def stage5():
            swap.wait_recv()
            mine = pl.ds(pl.multiple_of(base + p2 * mid, mid), mid)
            full[mine, cols] = (q2[:, cols] + zin[:, cols]) * (1.0 / (ns * NZ * NX * NY))
            g2()

        def stage7():
            i2()
            g1()

        def stage9():
            i1()
            if edge:
                half = size // 2
                dst = [(col, 0, half), (col + half, own - half, half)]
            else:
                dst = [(col, col + width, size)]
            for k, (a, b, w) in enumerate(dst):
                d = pltpu.make_async_copy(
                    full.at[:, pl.ds(a, w)], out.at[:, pl.ds(b, w)], osem.at[c + k])
                d.start()
                outs.append(d)

        return (stage0, b1r, b1l, stage2, b2r, b2l, stage4, stage5, h2r, h2l, stage7, h1r, h1l, stage9)

    outs = []
    work = [chunk(c, *spec) for c, spec in enumerate(chunks)]
    for code in ORDER:
        work[code % 8][code // 8]()
    for d in sends:
        d.wait_send()
    pl.when(upper)(lambda: edge_sent(True))
    pl.when(lower)(lambda: edge_sent(False))
    for d in outs:
        d.wait()


def reduce(partial, own_edge, out_edge, hits, n):
    nt, own = partial.shape
    _, ns, _, width = own_edge.shape
    pairs = 4
    size = own // (2 * pairs)
    chunks = tuple((k * size, size, k % 2) for k in range(2 * pairs - 1))
    chunks += (((2 * pairs - 1) * size, size, None),)

    def rows(k):
        return pltpu.VMEM((k, own), F32)

    sem = pltpu.SemaphoreType.DMA
    return pl.pallas_call(
        functools.partial(reduce_kernel, n, chunks),
        out_shape=(
            jax.ShapeDtypeStruct((nt, own), F32),
            jax.ShapeDtypeStruct((2, ns, nt, width), BF16),
        ),
        in_specs=[VM] * 4,
        out_specs=(ANY, VM),
        scratch_shapes=[
            rows(nt),
            pltpu.VMEM((nt, size), F32),
            pltpu.VMEM((2, ns, nt, width), F32),
            pltpu.VMEM((2, 8, width), F32),
            rows(nt // 4), rows(nt // 2), rows(nt // 4), rows(nt // 4),
            rows(nt // 16), rows(nt // 8), rows(nt // 16), rows(nt // 16), rows(nt // 16),
            sem((2 * pairs, SENDS)), sem((2 * pairs, SENDS)), sem((2, 4)), sem((2 * pairs + 1,)),
        ],
        compiler_params=pltpu.CompilerParams(
            collective_id=1, has_side_effects=True, vmem_limit_bytes=20 << 20),
        name="reduce",
    )(partial, own_edge, out_edge, hits)


def finish_kernel(aligned_in, edge_aligned, template_in, aligned, template, sem):
    own = aligned.shape[2]
    width = edge_aligned.shape[3]
    stores = [pltpu.make_async_copy(template_in, template, sem.at[2])]
    for side in range(2):
        cols = pl.ds(0 if side == 0 else own - width, width)
        stores.append(pltpu.make_async_copy(
            edge_aligned.at[side], aligned.at[:, :, cols], sem.at[side]))
    for c in stores:
        c.start()
    for c in stores:
        c.wait()


def finish(aligned, edge_aligned, template):
    return pl.pallas_call(
        finish_kernel,
        out_shape=(
            jax.ShapeDtypeStruct(aligned.shape, aligned.dtype),
            jax.ShapeDtypeStruct(template.shape, template.dtype),
        ),
        in_specs=[HBM, VM, VM],
        out_specs=(HBM, HBM),
        scratch_shapes=[pltpu.SemaphoreType.DMA((3,))],
        input_output_aliases={0: 0},
        compiler_params=pltpu.CompilerParams(vmem_limit_bytes=8 << 20),
        name="finish",
    )(aligned, edge_aligned, template)


def local(n, data, template, centres, neighbours):
    width = neighbours.shape[1]
    wide = halos(data, template, n, width)
    aligned, partial, own_edge, out_edge, hits = align(centres, neighbours, wide, data.shape)
    new_template, edge_aligned = reduce(partial, own_edge, out_edge, hits, n)
    return finish(aligned, edge_aligned, new_template)


def solution(mesh):
    in_specs = (P("subj", None, "vert"), P(None, "vert"), P("vert"), P("vert", None))
    out_specs = (P("subj", None, "vert"), P(None, "vert"))
    return jax.shard_map(
        functools.partial(local, mesh.shape["vert"]), mesh=mesh,
        in_specs=in_specs, out_specs=out_specs, check_vma=False)
```

```python
import functools

import jax
import jax.numpy as jnp
from jax import lax
from jax.experimental import pallas as pl
from jax.experimental.pallas import tpu as pltpu
from jax.sharding import PartitionSpec as P

NS_STEPS = 4
UNROLL = 4
MESH = pl.DeviceIdType.MESH
ANY = pl.BlockSpec(memory_space=pl.ANY)
VM = pl.BlockSpec(memory_space=pltpu.VMEM)
HBM = pl.BlockSpec(memory_space=pltpu.HBM)
SM = pl.BlockSpec(memory_space=pltpu.SMEM)
F32, BF16 = jnp.float32, jnp.bfloat16
LANES = 128


def dot(a, b, dims):
    return lax.dot_general(a, b, (dims, ((), ())), preferred_element_type=F32)


NN, NT, TN = ((1,), (0,)), ((1,), (1,)), ((0,), (0,))


def pieces(x):
    hi = x.astype(BF16)
    return hi, (x - hi.astype(F32)).astype(BF16)


def halo_kernel(n, data, tmpl, wide, lsem, ssem, rsem):
    v = lax.axis_index("vert")
    ns, nt, own = data.shape
    width = (wide.shape[1] - own) // 2
    barrier = pltpu.get_barrier_semaphore()
    lower, upper = v > 0, v < n - 1

    def greet(other):
        pl.semaphore_signal(barrier, inc=1, device_id={"vert": other}, device_id_type=MESH)

    def rows(i):
        return pl.ds(i * nt, nt)

    def src(i, cols):
        return data.at[i, :, cols] if i < ns else tmpl.at[:, cols]

    pl.when(lower)(lambda: greet(v - 1))
    pl.when(upper)(lambda: greet(v + 1))
    mine = [
        pltpu.make_async_copy(
            src(i, pl.ds(0, own)), wide.at[rows(i), pl.ds(width, own)], lsem.at[i])
        for i in range(ns + 1)
    ]
    for c in mine:
        c.start()
    pl.semaphore_wait(barrier, jnp.minimum(v, 1) + jnp.minimum(n - 1 - v, 1))

    def copies(up):
        cols = pl.ds(own - width, width) if up else pl.ds(0, width)
        dst = pl.ds(0, width) if up else pl.ds(width + own, width)
        to = {"vert": v + 1 if up else v - 1}
        k = 0 if up else ns + 1
        return [
            pltpu.make_async_remote_copy(
                src(i, cols), wide.at[rows(i), dst], ssem.at[k + i], rsem.at[k + i],
                device_id=to, device_id_type=MESH)
            for i in range(ns + 1)
        ]

    def start(up):
        for c in copies(up):
            c.start()

    def sent(up):
        for c in copies(up):
            c.wait_send()

    def received(up):
        for c in copies(up):
            c.wait_recv()

    def blank(at):
        wide[:, pl.ds(at, width)] = jnp.zeros((wide.shape[0], width), wide.dtype)

    pl.when(upper)(lambda: start(True))
    pl.when(lower)(lambda: start(False))
    pl.when(jnp.logical_not(lower))(lambda: blank(0))
    pl.when(jnp.logical_not(upper))(lambda: blank(width + own))
    for c in mine:
        c.wait()
    pl.when(upper)(lambda: sent(True))
    pl.when(lower)(lambda: sent(False))
    pl.when(lower)(lambda: received(True))
    pl.when(upper)(lambda: received(False))


def halos(data, template, n, width):
    ns, nt, own = data.shape
    sem = pltpu.SemaphoreType.DMA
    return pl.pallas_call(
        functools.partial(halo_kernel, n),
        out_shape=jax.ShapeDtypeStruct(((ns + 1) * nt, own + 2 * width), data.dtype),
        in_specs=[HBM, HBM],
        out_specs=VM,
        scratch_shapes=[sem((ns + 1,)), sem((2 * ns + 2,)), sem((2 * ns + 2,))],
        compiler_params=pltpu.CompilerParams(
            collective_id=0, has_side_effects=True, vmem_limit_bytes=8 << 20),
        name="halo",
    )(*(pltpu.with_memory_space_constraint(a, pltpu.HBM) for a in (data, template)))


def align_kernel(ns, unroll, cen, nb, wide, aligned, partial, acc, xbuf, zbuf, ybuf):
    lights, width = nb.shape
    nt, own = partial.shape
    tiles = own // LANES
    groups = lights // unroll
    lane = lax.broadcasted_iota(jnp.int32, (1, LANES), 1)

    def rows(i):
        return pl.ds(i * nt, nt)

    acc[...] = jnp.zeros_like(acc)
    ones = jnp.ones((16, width), BF16)
    none = jnp.zeros((16, width), BF16)

    def window(c):
        local = lax.rem(cen[c], own)
        base = pl.multiple_of(lax.div(local, LANES) * LANES, LANES)
        target = nb[pl.ds(c, 1), :] + width
        pick = (lax.broadcasted_iota(jnp.int32, (2 * LANES, width), 0) == target)
        return base, local - base, pick.astype(F32).astype(BF16)

    def gather(g):
        for u in range(unroll):
            base, off, pick = window(g * unroll + u)
            back = lax.rem(LANES - off, LANES)
            kept = lane < LANES - off
            x = []
            for i in range(ns + 1):
                p, q, r = (
                    pltpu.roll(wide[rows(i), pl.ds(base + k * LANES, LANES)], back, 1)
                    for k in range(3))
                seen = jnp.concatenate([jnp.where(kept, p, q), jnp.where(kept, q, r)], axis=1)
                x.append(dot(seen, pick, NN).astype(BF16))
                yield
            m = x.pop()
            for i in range(ns):
                xbuf[lax.rem(g, 3), u * ns + i] = x[i]
            both = dot(m, jnp.concatenate(x, axis=1), TN)
            for i in range(ns):
                z = both[:, i * width:(i + 1) * width]
                norm = jnp.sum(z * z, axis=(0, 1), keepdims=True)
                zbuf[lax.rem(g, 2), u * ns + i] = z * (1.0 / jnp.sqrt(norm + 1e-06))
            yield

    def iterate(g):
        zs = [zbuf[lax.rem(g, 2), k] for k in range(unroll * ns)]
        for step in range(NS_STEPS):
            grams = []
            for z in zs:
                zh, zl = pieces(z)
                a = jnp.concatenate([zh, zl], axis=1)
                b = jnp.concatenate(
                    [jnp.concatenate([zh, zh], axis=1), jnp.concatenate([zl, zl], axis=1)], axis=0)
                p = dot(a, b, NT)
                grams.append((p[:, :width] + p[:, width:], zh, zl))
                yield
            nxt = []
            for z, (gram, zh, zl) in zip(zs, grams):
                gh, gl = pieces(gram)
                a = jnp.concatenate([gh, gl], axis=1)
                b = jnp.concatenate([zh, zl], axis=1)
                p = dot(a, jnp.concatenate([b, b], axis=0), NN)
                nxt.append(1.5 * z - 0.5 * (p[:, :width] + p[:, width:]))
                yield
            zs = nxt
        for k, z in enumerate(zs):
            ybuf[lax.rem(g, 2), k] = jnp.concatenate(pieces(z), axis=1)

    def scatter(g):
        for u in range(unroll):
            base, off, pick = window(g * unroll + u)
            parts = []
            for i in range(ns):
                x = xbuf[lax.rem(g, 3), u * ns + i]
                turned = dot(
                    jnp.concatenate([x, x], axis=1), ybuf[lax.rem(g, 2), u * ns + i], NT)
                parts.append(jnp.concatenate(pieces(turned), axis=1))
                yield
            parts[-1] = jnp.concatenate([parts[-1], jnp.concatenate([ones, none], axis=1)], axis=0)
            twice = jnp.concatenate([pick, pick], axis=1)
            inside = lane >= off
            for i in range(ns):
                spread = dot(parts[i], twice, NT)
                at = pl.ds(i * nt, spread.shape[0])
                p, q = (pltpu.roll(spread[:, k * LANES:(k + 1) * LANES], off, 1) for k in range(2))
                acc[at, pl.ds(base, LANES)] += jnp.where(inside, p, 0.0)
                acc[at, pl.ds(base + LANES, LANES)] += jnp.where(inside, q, p)
                acc[at, pl.ds(base + 2 * LANES, LANES)] += jnp.where(inside, 0.0, q)
                yield

    def together(*works):
        works = [[w, n, 0] for w, n in works]
        while works:
            w = min(works, key=lambda w: (w[2] + 0.5) / w[1])
            w[2] += 1
            if next(w[0], works) is works:
                works.remove(w)

    def gathering(g):
        return gather(g), unroll * (ns + 2)

    def iterating(g):
        return iterate(g), 2 * NS_STEPS * unroll * ns

    def scattering(g):
        return scatter(g), unroll * 2 * ns

    def body(g, _):
        together(scattering(g - 1), iterating(g), gathering(g + 1))
        return 0

    together(gathering(0))
    together(iterating(0), gathering(1))
    lax.fori_loop(1, groups - 1, body, 0)
    together(scattering(groups - 2), iterating(groups - 1))
    together(scattering(groups - 1))
    for t in range(1, tiles - 1):
        src = pl.ds((t + 1) * LANES, LANES)
        dst = pl.ds(t * LANES, LANES)
        inv = 1.0 / jnp.maximum(acc[pl.ds(ns * nt, 1), src], 1.0)
        total = None
        for i in range(ns):
            mapped = acc[rows(i), src] * inv
            aligned[i, :, dst] = mapped.astype(BF16)
            total = mapped if total is None else total + mapped
        partial[:, pl.ds((t - 1) * LANES, LANES)] = total


def align(centres, neighbours, wide, shape):
    ns, nt, own = shape
    width = neighbours.shape[1]
    return pl.pallas_call(
        functools.partial(align_kernel, ns, UNROLL),
        out_shape=(
            jax.ShapeDtypeStruct(shape, BF16),
            jax.ShapeDtypeStruct((nt, own), F32),
            jax.ShapeDtypeStruct((ns * nt + 16, wide.shape[1]), F32),
        ),
        in_specs=[SM, VM, VM],
        out_specs=(VM,) * 3,
        scratch_shapes=[
            pltpu.VMEM((3, UNROLL * ns, nt, width), BF16),
            pltpu.VMEM((2, UNROLL * ns, width, width), F32),
            pltpu.VMEM((2, UNROLL * ns, width, 2 * width), BF16),
        ],
        compiler_params=pltpu.CompilerParams(vmem_limit_bytes=24 << 20),
        name="align",
    )(centres, neighbours, wide)


NZ, NX, NY = 2, 4, 4
ORDER = (
    0, 1, 2, 3, 4, 5, 16, 17, 8, 9, 18, 19, 10, 11, 6, 7,
    20, 21, 12, 13, 24, 25, 26, 27, 22, 23, 14, 15, 28, 29, 41, 40,
    32, 43, 42, 33, 34, 35, 30, 31, 44, 45, 36, 37, 48, 49, 50, 51,
    46, 47, 38, 39, 52, 53, 54, 55, 56, 57, 72, 64, 58, 73, 65, 59,
    80, 74, 66, 60, 81, 75, 67, 61, 82, 96, 76, 88, 68, 62, 83, 97,
    77, 89, 69, 63, 84, 98, 78, 90, 70, 104, 85, 99, 79, 91, 71, 105,
    86, 100, 92, 106, 87, 101, 93, 107, 102, 94, 108, 103, 95, 109, 110, 111,
)
RS, AG = 6, 4
SENDS = 2 * RS + 1 + 2 * AG


def reduce_kernel(n, ns, chunks, part, sums, out, edge_aligned, full, edge_part, edge_in, r1, r2, t1, q1, s1, s2, u1, q2, zin,
                  ssem, rsem, esem, osem):
    s, v = lax.axis_index("subj"), lax.axis_index("vert")
    nt, own = full.shape
    width = edge_in.shape[2]
    y, x, zh = lax.rem(s, NY), lax.rem(lax.div(s, NY), NX), lax.div(s, NX * NY)

    def place(zh, x, y):
        return {"subj": (zh * NX + x) * NY + y}

    def along(axis, by):
        if axis == 0:
            return place(zh, lax.rem(x + by + NX, NX), y)
        return place(zh, x, lax.rem(y + by + NY, NY))

    across = place(NZ - 1 - zh, x, y)
    barrier = pltpu.get_barrier_semaphore()
    lower, upper = v > 0, v < n - 1

    def greet(to):
        pl.semaphore_signal(barrier, inc=1, device_id=to, device_id_type=MESH)

    for to in (along(0, 1), along(0, -1), along(1, 1), along(1, -1), across):
        greet(to)
    pl.when(lower)(lambda: greet({"vert": v - 1}))
    pl.when(upper)(lambda: greet({"vert": v + 1}))
    pl.semaphore_wait(barrier, 5 + jnp.minimum(v, 1) + jnp.minimum(n - 1 - v, 1))

    def edge_copy(up):
        k = 1 if up else 0
        cols = pl.ds(width + own, width) if up else pl.ds(0, width)
        return pltpu.make_async_remote_copy(
            sums.at[pl.ds(0, ns * nt + 8), cols], edge_in.at[k], esem.at[0, k], esem.at[1, k],
            device_id={"vert": v + 1 if up else v - 1}, device_id_type=MESH)

    def edge_start(up):
        edge_copy(up).start()

    def edge_sent(up):
        edge_copy(up).wait_send()

    def edge_got(up):
        edge_copy(up).wait_recv()

    def edge_blank(up):
        k = 1 if up else 0
        edge_in[k] = jnp.zeros(edge_in.shape[1:], F32)

    pl.when(upper)(lambda: edge_start(True))
    pl.when(lower)(lambda: edge_start(False))
    pl.when(jnp.logical_not(lower))(lambda: edge_blank(True))
    pl.when(jnp.logical_not(upper))(lambda: edge_blank(False))

    def edges():
        pl.when(lower)(lambda: edge_got(True))
        pl.when(upper)(lambda: edge_got(False))
        for side in range(2):
            k = 1 - side
            at = pl.ds(width if side == 0 else own, width)
            count = sums[pl.ds(ns * nt, 1), at] + edge_in[k, pl.ds(ns * nt, 1), :]
            inv = 1.0 / jnp.maximum(count, 1.0)
            total = None
            for i in range(ns):
                mine = pl.ds(i * nt, nt)
                mapped = (sums[mine, at] + edge_in[k, mine, :]) * inv
                edge_aligned[side, i] = mapped.astype(BF16)
                total = mapped if total is None else total + mapped
            edge_part[:, side * width:(side + 1) * width] = total

    sends = []

    def rs_stages(c, first, axis, p, src, cols, half, r1, r2, t, dst):
        right, left = along(axis, 1), along(axis, -1)

        def go(k, a, b, to):
            d = pltpu.make_async_remote_copy(
                a, b, ssem.at[c, first + k], rsem.at[c, first + k],
                device_id=to, device_id_type=MESH)
            d.start()
            sends.append(d)

        def got(k, b):
            pltpu.make_async_remote_copy(
                b, b, ssem.at[c, first + k], rsem.at[c, first + k],
                device_id=right, device_id_type=MESH).wait_recv()

        def slot(ref, k):
            return ref.at[pl.ds(k * half, half), cols]

        def val(ref, k):
            return ref[pl.ds(k * half, half), cols]

        nxt, far, prv = lax.rem(p + 1, 4), lax.rem(p + 2, 4), lax.rem(p + 3, 4)

        def at(q, h):
            ref, rows, cc = src(q, h)
            return ref.at[rows, cc]

        def load(q, h):
            ref, rows, cc = src(q, h)
            return ref[rows, cc]

        def a():
            go(0, at(far, 0), slot(r1, 0), right)
            go(1, at(far, 1), slot(r1, 1), left)
            go(2, at(nxt, 1), slot(r2, 1), right)
            go(3, at(prv, 0), slot(r2, 2), left)

        def b_right():
            got(0, slot(r1, 0))
            t[pl.ds(0, half), cols] = load(nxt, 0) + val(r1, 0)
            go(4, slot(t, 0), slot(r2, 0), right)

        def b_left():
            got(1, slot(r1, 1))
            t[pl.ds(half, half), cols] = load(prv, 1) + val(r1, 1)
            go(5, slot(t, 1), slot(r2, 3), left)

        def c_():
            got(3, slot(r2, 2))
            got(4, slot(r2, 0))
            dst[pl.ds(0, half), cols] = load(p, 0) + (val(r2, 0) + val(r2, 2))
            got(2, slot(r2, 1))
            got(5, slot(r2, 3))
            dst[pl.ds(half, half), cols] = load(p, 1) + (val(r2, 1) + val(r2, 3))

        return a, b_right, b_left, c_

    def ag_stages(c, first, axis, p, piece):
        right, left = along(axis, 1), along(axis, -1)
        nxt, far, prv = lax.rem(p + 1, 4), lax.rem(p + 2, 4), lax.rem(p + 3, 4)

        def desc(k, ref, to):
            return pltpu.make_async_remote_copy(
                ref, ref, ssem.at[c, first + k], rsem.at[c, first + k],
                device_id=to, device_id_type=MESH)

        def go(k, ref, to):
            d = desc(k, ref, to)
            d.start()
            sends.append(d)

        def a():
            go(0, piece(p, None), right)
            go(1, piece(p, None), left)

        def b_right():
            desc(0, piece(prv, None), right).wait_recv()
            go(2, piece(prv, 0), right)

        def b_left():
            desc(1, piece(nxt, None), right).wait_recv()
            go(3, piece(nxt, 1), left)

        def c_():
            desc(2, piece(far, 0), right).wait_recv()
            desc(3, piece(far, 1), right).wait_recv()

        return a, b_right, b_left, c_

    big, mid, small = nt // 4, nt // 16, nt // 32

    def chunk(c, col, size, order):
        edge = order is None
        first = 1 if edge else order
        second = 1 - first
        pos = (x, y)
        p1, p2 = pos[first], pos[second]
        cols = pl.ds(col, size)

        def rows(q, h, unit, base=0):
            start = base + q * unit
            if h is None:
                return pl.ds(pl.multiple_of(start, unit), unit)
            return pl.ds(pl.multiple_of(start + h * (unit // 2), unit // 2), unit // 2)

        def src1(q, h):
            if edge:
                return edge_part, rows(q, h, big), pl.ds(0, size)
            return part, rows(q, h, big), cols

        def src2(q, h):
            return q1, rows(q, h, mid), cols

        a1, b1r, b1l, c1 = rs_stages(c, 0, first, p1, src1, cols, big // 2, r1, r2, t1, q1)
        a2, b2r, b2l, c2 = rs_stages(c, RS, second, p2, src2, cols, mid // 2, s1, s2, u1, q2)
        base = p1 * big

        def piece2(q, h):
            return full.at[rows(q, h, mid, base), cols]

        def piece1(q, h):
            return full.at[rows(q, h, big), cols]

        g2, h2r, h2l, i2 = ag_stages(c, 2 * RS + 1, second, p2, piece2)
        g1, h1r, h1l, i1 = ag_stages(c, 2 * RS + 1 + AG, first, p1, piece1)
        kz = 2 * RS
        swap = pltpu.make_async_remote_copy(
            q2.at[:, cols], zin.at[:, cols], ssem.at[c, kz], rsem.at[c, kz],
            device_id=across, device_id_type=MESH)

        def stage0():
            if edge:
                edges()
            a1()

        def stage2():
            c1()
            a2()

        def stage4():
            c2()
            swap.start()
            sends.append(swap)

        def stage5():
            swap.wait_recv()
            mine = pl.ds(pl.multiple_of(base + p2 * mid, mid), mid)
            full[mine, cols] = (q2[:, cols] + zin[:, cols]) * (1.0 / (ns * NZ * NX * NY))
            g2()

        def stage7():
            i2()
            g1()

        def stage9():
            i1()
            if edge:
                half = size // 2
                dst = [(col, 0, half), (col + half, own - half, half)]
            else:
                dst = [(col, col + width, size)]
            for k, (a, b, w) in enumerate(dst):
                d = pltpu.make_async_copy(
                    full.at[:, pl.ds(a, w)], out.at[:, pl.ds(b, w)], osem.at[c + k])
                d.start()
                outs.append(d)

        return (stage0, b1r, b1l, stage2, b2r, b2l, stage4, stage5, h2r, h2l, stage7, h1r, h1l, stage9)

    outs = []
    work = [chunk(c, *spec) for c, spec in enumerate(chunks)]
    for code in ORDER:
        work[code % 8][code // 8]()
    for d in sends:
        d.wait_send()
    pl.when(upper)(lambda: edge_sent(True))
    pl.when(lower)(lambda: edge_sent(False))
    for d in outs:
        d.wait()


def reduce(partial, sums, ns, width, n):
    nt, own = partial.shape
    pairs = 4
    size = own // (2 * pairs)
    chunks = tuple((k * size, size, k % 2) for k in range(2 * pairs - 1))
    chunks += (((2 * pairs - 1) * size, size, None),)

    def rows(k):
        return pltpu.VMEM((k, own), F32)

    sem = pltpu.SemaphoreType.DMA
    return pl.pallas_call(
        functools.partial(reduce_kernel, n, ns, chunks),
        out_shape=(
            jax.ShapeDtypeStruct((nt, own), F32),
            jax.ShapeDtypeStruct((2, ns, nt, width), BF16),
        ),
        in_specs=[VM] * 2,
        out_specs=(ANY, VM),
        scratch_shapes=[
            rows(nt),
            pltpu.VMEM((nt, size), F32),
            pltpu.VMEM((2, ns * nt + 8, width), F32),
            rows(nt // 4), rows(nt // 2), rows(nt // 4), rows(nt // 4),
            rows(nt // 16), rows(nt // 8), rows(nt // 16), rows(nt // 16), rows(nt // 16),
            sem((2 * pairs, SENDS)), sem((2 * pairs, SENDS)), sem((2, 2)), sem((2 * pairs + 1,)),
        ],
        compiler_params=pltpu.CompilerParams(
            collective_id=1, has_side_effects=True, vmem_limit_bytes=20 << 20),
        name="reduce",
    )(partial, sums)


def finish_kernel(aligned_in, edge_aligned, template_in, aligned, template, sem):
    own = aligned.shape[2]
    width = edge_aligned.shape[3]
    stores = [pltpu.make_async_copy(template_in, template, sem.at[2])]
    for side in range(2):
        cols = pl.ds(0 if side == 0 else own - width, width)
        stores.append(pltpu.make_async_copy(
            edge_aligned.at[side], aligned.at[:, :, cols], sem.at[side]))
    for c in stores:
        c.start()
    for c in stores:
        c.wait()


def finish(aligned, edge_aligned, template):
    return pl.pallas_call(
        finish_kernel,
        out_shape=(
            jax.ShapeDtypeStruct(aligned.shape, aligned.dtype),
            jax.ShapeDtypeStruct(template.shape, template.dtype),
        ),
        in_specs=[HBM, VM, VM],
        out_specs=(HBM, HBM),
        scratch_shapes=[pltpu.SemaphoreType.DMA((3,))],
        input_output_aliases={0: 0},
        compiler_params=pltpu.CompilerParams(vmem_limit_bytes=8 << 20),
        name="finish",
    )(aligned, edge_aligned, template)


def local(n, data, template, centres, neighbours):
    width = neighbours.shape[1]
    wide = halos(data, template, n, width)
    aligned, partial, sums = align(centres, neighbours, wide, data.shape)
    new_template, edge_aligned = reduce(partial, sums, data.shape[0], width, n)
    return finish(aligned, edge_aligned, new_template)


def solution(mesh):
    in_specs = (P("subj", None, "vert"), P(None, "vert"), P("vert"), P("vert", None))
    out_specs = (P("subj", None, "vert"), P(None, "vert"))
    return jax.shard_map(
        functools.partial(local, mesh.shape["vert"]), mesh=mesh,
        in_specs=in_specs, out_specs=out_specs, check_vma=False)
```

```python
import functools

import jax
import jax.numpy as jnp
from jax import lax
from jax.experimental import pallas as pl
from jax.experimental.pallas import tpu as pltpu
from jax.sharding import PartitionSpec as P

NS_STEPS = 4
UNROLL = 4
MESH = pl.DeviceIdType.MESH
ANY = pl.BlockSpec(memory_space=pl.ANY)
VM = pl.BlockSpec(memory_space=pltpu.VMEM)
HBM = pl.BlockSpec(memory_space=pltpu.HBM)
SM = pl.BlockSpec(memory_space=pltpu.SMEM)
F32, BF16 = jnp.float32, jnp.bfloat16
LANES = 128


def dot(a, b, dims):
    return lax.dot_general(a, b, (dims, ((), ())), preferred_element_type=F32)


NN, NT, TN = ((1,), (0,)), ((1,), (1,)), ((0,), (0,))


def pieces(x):
    hi = x.astype(BF16)
    return hi, (x - hi.astype(F32)).astype(BF16)


def halo_kernel(n, data, tmpl, wide, lsem, ssem, rsem):
    v = lax.axis_index("vert")
    ns, nt, own = data.shape
    width = (wide.shape[1] - own) // 2
    barrier = pltpu.get_barrier_semaphore()
    lower, upper = v > 0, v < n - 1

    def greet(other):
        pl.semaphore_signal(barrier, inc=1, device_id={"vert": other}, device_id_type=MESH)

    def rows(i):
        return pl.ds(i * nt, nt)

    def src(i, cols):
        return data.at[i, :, cols] if i < ns else tmpl.at[:, cols]

    pl.when(lower)(lambda: greet(v - 1))
    pl.when(upper)(lambda: greet(v + 1))
    mine = [
        pltpu.make_async_copy(
            src(i, pl.ds(0, own)), wide.at[rows(i), pl.ds(width, own)], lsem.at[i])
        for i in range(ns + 1)
    ]
    for c in mine:
        c.start()
    pl.semaphore_wait(barrier, jnp.minimum(v, 1) + jnp.minimum(n - 1 - v, 1))

    def copies(up):
        cols = pl.ds(own - width, width) if up else pl.ds(0, width)
        dst = pl.ds(0, width) if up else pl.ds(width + own, width)
        to = {"vert": v + 1 if up else v - 1}
        k = 0 if up else ns + 1
        return [
            pltpu.make_async_remote_copy(
                src(i, cols), wide.at[rows(i), dst], ssem.at[k + i], rsem.at[k + i],
                device_id=to, device_id_type=MESH)
            for i in range(ns + 1)
        ]

    def start(up):
        for c in copies(up):
            c.start()

    def sent(up):
        for c in copies(up):
            c.wait_send()

    def received(up):
        for c in copies(up):
            c.wait_recv()

    def blank(at):
        wide[:, pl.ds(at, width)] = jnp.zeros((wide.shape[0], width), wide.dtype)

    pl.when(upper)(lambda: start(True))
    pl.when(lower)(lambda: start(False))
    pl.when(jnp.logical_not(lower))(lambda: blank(0))
    pl.when(jnp.logical_not(upper))(lambda: blank(width + own))
    for c in mine:
        c.wait()
    pl.when(upper)(lambda: sent(True))
    pl.when(lower)(lambda: sent(False))
    pl.when(lower)(lambda: received(True))
    pl.when(upper)(lambda: received(False))


def halos(data, template, n, width):
    ns, nt, own = data.shape
    sem = pltpu.SemaphoreType.DMA
    return pl.pallas_call(
        functools.partial(halo_kernel, n),
        out_shape=jax.ShapeDtypeStruct(((ns + 1) * nt, own + 2 * width), data.dtype),
        in_specs=[HBM, HBM],
        out_specs=VM,
        scratch_shapes=[sem((ns + 1,)), sem((2 * ns + 2,)), sem((2 * ns + 2,))],
        compiler_params=pltpu.CompilerParams(
            collective_id=0, has_side_effects=True, vmem_limit_bytes=8 << 20),
        name="halo",
    )(*(pltpu.with_memory_space_constraint(a, pltpu.HBM) for a in (data, template)))


def align_kernel(ns, unroll, cen, nb, wide, aligned, partial, acc, xbuf, zbuf, ybuf):
    lights, width = nb.shape
    nt, own = partial.shape
    tiles = own // LANES
    groups = lights // unroll
    lane = lax.broadcasted_iota(jnp.int32, (1, LANES), 1)

    def rows(i):
        return pl.ds(i * nt, nt)

    acc[...] = jnp.zeros_like(acc)
    ones = jnp.ones((16, width), BF16)
    none = jnp.zeros((16, width), BF16)

    def window(c):
        local = lax.rem(cen[c], own)
        base = pl.multiple_of(lax.div(local, LANES) * LANES, LANES)
        target = nb[pl.ds(c, 1), :] + width
        pick = (lax.broadcasted_iota(jnp.int32, (2 * LANES, width), 0) == target)
        return base, local - base, pick.astype(F32).astype(BF16)

    def gather(g):
        for u in range(unroll):
            base, off, pick = window(g * unroll + u)
            back = lax.rem(LANES - off, LANES)
            kept = lane < LANES - off
            x = []
            for i in range(ns + 1):
                p, q, r = (
                    pltpu.roll(wide[rows(i), pl.ds(base + k * LANES, LANES)], back, 1)
                    for k in range(3))
                seen = jnp.concatenate([jnp.where(kept, p, q), jnp.where(kept, q, r)], axis=1)
                x.append(dot(seen, pick, NN).astype(BF16))
                yield
            m = x.pop()
            for i in range(ns):
                xbuf[lax.rem(g, 3), u * ns + i] = x[i]
            both = dot(m, jnp.concatenate(x, axis=1), TN)
            for i in range(ns):
                z = both[:, i * width:(i + 1) * width]
                norm = jnp.sum(z * z, axis=(0, 1), keepdims=True)
                zbuf[lax.rem(g, 2), u * ns + i] = z * (1.0 / jnp.sqrt(norm + 1e-06))
            yield

    def iterate(g):
        zs = [zbuf[lax.rem(g, 2), k] for k in range(unroll * ns)]
        for step in range(NS_STEPS):
            grams = []
            for z in zs:
                zh, zl = pieces(z)
                a = jnp.concatenate([zh, zl], axis=1)
                b = jnp.concatenate(
                    [jnp.concatenate([zh, zh], axis=1), jnp.concatenate([zl, zl], axis=1)], axis=0)
                p = dot(a, b, NT)
                grams.append((p[:, :width] + p[:, width:], zh, zl))
                yield
            nxt = []
            for z, (gram, zh, zl) in zip(zs, grams):
                gh, gl = pieces(gram)
                a = jnp.concatenate([gh, gl], axis=1)
                b = jnp.concatenate([zh, zl], axis=1)
                p = dot(a, jnp.concatenate([b, b], axis=0), NN)
                nxt.append(1.5 * z - 0.5 * (p[:, :width] + p[:, width:]))
                yield
            zs = nxt
        for k, z in enumerate(zs):
            ybuf[lax.rem(g, 2), k] = jnp.concatenate(pieces(z), axis=1)

    def scatter(g):
        for u in range(unroll):
            base, off, pick = window(g * unroll + u)
            parts = []
            for i in range(ns):
                x = xbuf[lax.rem(g, 3), u * ns + i]
                turned = dot(
                    jnp.concatenate([x, x], axis=1), ybuf[lax.rem(g, 2), u * ns + i], NT)
                parts.append(jnp.concatenate(pieces(turned), axis=1))
                yield
            parts[-1] = jnp.concatenate([parts[-1], jnp.concatenate([ones, none], axis=1)], axis=0)
            twice = jnp.concatenate([pick, pick], axis=1)
            inside = lane >= off
            for i in range(ns):
                spread = dot(parts[i], twice, NT)
                at = pl.ds(i * nt, spread.shape[0])
                p, q = (pltpu.roll(spread[:, k * LANES:(k + 1) * LANES], off, 1) for k in range(2))
                acc[at, pl.ds(base, LANES)] += jnp.where(inside, p, 0.0)
                acc[at, pl.ds(base + LANES, LANES)] += jnp.where(inside, q, p)
                acc[at, pl.ds(base + 2 * LANES, LANES)] += jnp.where(inside, 0.0, q)
                yield

    def together(*works):
        works = [[w, n, 0] for w, n in works]
        while works:
            w = min(works, key=lambda w: (w[2] + 0.5) / w[1])
            w[2] += 1
            if next(w[0], works) is works:
                works.remove(w)

    def gathering(g):
        return gather(g), unroll * (ns + 2)

    def iterating(g):
        return iterate(g), 2 * NS_STEPS * unroll * ns

    def scattering(g):
        return scatter(g), unroll * 2 * ns

    def body(g, _):
        together(scattering(g - 1), iterating(g), gathering(g + 1))
        return 0

    together(gathering(0))
    together(iterating(0), gathering(1))
    lax.fori_loop(1, groups - 1, body, 0)
    together(scattering(groups - 2), iterating(groups - 1))
    together(scattering(groups - 1))
    for t in range(1, tiles - 1):
        src = pl.ds((t + 1) * LANES, LANES)
        dst = pl.ds(t * LANES, LANES)
        inv = 1.0 / jnp.maximum(acc[pl.ds(ns * nt, 1), src], 1.0)
        total = None
        for i in range(ns):
            mapped = acc[rows(i), src] * inv
            aligned[i, :, dst] = mapped.astype(BF16)
            total = mapped if total is None else total + mapped
        partial[:, pl.ds((t - 1) * LANES, LANES)] = total


def align(centres, neighbours, wide, shape):
    ns, nt, own = shape
    width = neighbours.shape[1]
    return pl.pallas_call(
        functools.partial(align_kernel, ns, UNROLL),
        out_shape=(
            jax.ShapeDtypeStruct(shape, BF16),
            jax.ShapeDtypeStruct((nt, own), F32),
            jax.ShapeDtypeStruct((ns * nt + 16, wide.shape[1]), F32),
        ),
        in_specs=[SM, VM, VM],
        out_specs=(VM,) * 3,
        scratch_shapes=[
            pltpu.VMEM((3, UNROLL * ns, nt, width), BF16),
            pltpu.VMEM((2, UNROLL * ns, width, width), F32),
            pltpu.VMEM((2, UNROLL * ns, width, 2 * width), BF16),
        ],
        compiler_params=pltpu.CompilerParams(vmem_limit_bytes=24 << 20),
        name="align",
    )(centres, neighbours, wide)


NZ, NX, NY = 2, 4, 4
WIDTHS = (256, 256, 256, 256, 256, 256, 256, 256)
ORDER = (
    0, 1, 2, 3, 4, 5, 6, 7, 16, 17, 8, 9, 18, 19, 10, 11,
    20, 12, 21, 13, 22, 14, 23, 15, 24, 25, 26, 27, 28, 29, 30, 31,
    40, 32, 41, 33, 42, 34, 43, 35, 44, 36, 45, 37, 46, 38, 47, 39,
    48, 49, 50, 51, 52, 53, 54, 55, 56, 57, 58, 59, 60, 61, 62, 63,
    72, 64, 73, 65, 74, 66, 75, 67, 76, 68, 77, 69, 78, 70, 79, 71,
    80, 81, 82, 83, 84, 85, 86, 87, 96, 88, 97, 89, 98, 90, 99, 91,
    100, 92, 101, 93, 102, 94, 103, 95, 104, 105, 106, 107, 108, 109, 110, 111,
)
RS, AG = 6, 4
SENDS = 2 * RS + 1 + 2 * AG


def reduce_kernel(n, ns, chunks, part, sums, out, edge_aligned, full, edge_part, edge_in, r1, r2, t1, q1, s1, s2, u1, q2, zin,
                  ssem, rsem, esem, osem):
    s, v = lax.axis_index("subj"), lax.axis_index("vert")
    nt, own = full.shape
    width = edge_in.shape[2]
    y, x, zh = lax.rem(s, NY), lax.rem(lax.div(s, NY), NX), lax.div(s, NX * NY)

    def place(zh, x, y):
        return {"subj": (zh * NX + x) * NY + y}

    def along(axis, by):
        if axis == 0:
            return place(zh, lax.rem(x + by + NX, NX), y)
        return place(zh, x, lax.rem(y + by + NY, NY))

    across = place(NZ - 1 - zh, x, y)
    barrier = pltpu.get_barrier_semaphore()
    lower, upper = v > 0, v < n - 1

    def greet(to):
        pl.semaphore_signal(barrier, inc=1, device_id=to, device_id_type=MESH)

    for to in (along(0, 1), along(0, -1), along(1, 1), along(1, -1), across):
        greet(to)
    pl.when(lower)(lambda: greet({"vert": v - 1}))
    pl.when(upper)(lambda: greet({"vert": v + 1}))
    pl.semaphore_wait(barrier, 5 + jnp.minimum(v, 1) + jnp.minimum(n - 1 - v, 1))

    def edge_copy(up):
        k = 1 if up else 0
        cols = pl.ds(width + own, width) if up else pl.ds(0, width)
        return pltpu.make_async_remote_copy(
            sums.at[pl.ds(0, ns * nt + 8), cols], edge_in.at[k], esem.at[0, k], esem.at[1, k],
            device_id={"vert": v + 1 if up else v - 1}, device_id_type=MESH)

    def edge_start(up):
        edge_copy(up).start()

    def edge_sent(up):
        edge_copy(up).wait_send()

    def edge_got(up):
        edge_copy(up).wait_recv()

    def edge_blank(up):
        k = 1 if up else 0
        edge_in[k] = jnp.zeros(edge_in.shape[1:], F32)

    pl.when(upper)(lambda: edge_start(True))
    pl.when(lower)(lambda: edge_start(False))
    pl.when(jnp.logical_not(lower))(lambda: edge_blank(True))
    pl.when(jnp.logical_not(upper))(lambda: edge_blank(False))

    def edges():
        pl.when(lower)(lambda: edge_got(True))
        pl.when(upper)(lambda: edge_got(False))
        for side in range(2):
            k = 1 - side
            at = pl.ds(width if side == 0 else own, width)
            count = sums[pl.ds(ns * nt, 1), at] + edge_in[k, pl.ds(ns * nt, 1), :]
            inv = 1.0 / jnp.maximum(count, 1.0)
            total = None
            for i in range(ns):
                mine = pl.ds(i * nt, nt)
                mapped = (sums[mine, at] + edge_in[k, mine, :]) * inv
                edge_aligned[side, i] = mapped.astype(BF16)
                total = mapped if total is None else total + mapped
            edge_part[:, side * width:(side + 1) * width] = total

    sends = []

    def rs_stages(c, first, axis, p, src, cols, half, r1, r2, t, dst):
        right, left = along(axis, 1), along(axis, -1)

        def go(k, a, b, to):
            d = pltpu.make_async_remote_copy(
                a, b, ssem.at[c, first + k], rsem.at[c, first + k],
                device_id=to, device_id_type=MESH)
            d.start()
            sends.append(d)

        def got(k, b):
            pltpu.make_async_remote_copy(
                b, b, ssem.at[c, first + k], rsem.at[c, first + k],
                device_id=right, device_id_type=MESH).wait_recv()

        def slot(ref, k):
            return ref.at[pl.ds(k * half, half), cols]

        def val(ref, k):
            return ref[pl.ds(k * half, half), cols]

        nxt, far, prv = lax.rem(p + 1, 4), lax.rem(p + 2, 4), lax.rem(p + 3, 4)

        def at(q, h):
            ref, rows, cc = src(q, h)
            return ref.at[rows, cc]

        def load(q, h):
            ref, rows, cc = src(q, h)
            return ref[rows, cc]

        def a():
            go(0, at(far, 0), slot(r1, 0), right)
            go(1, at(far, 1), slot(r1, 1), left)
            go(2, at(nxt, 1), slot(r2, 1), right)
            go(3, at(prv, 0), slot(r2, 2), left)

        def b_right():
            got(0, slot(r1, 0))
            t[pl.ds(0, half), cols] = load(nxt, 0) + val(r1, 0)
            go(4, slot(t, 0), slot(r2, 0), right)

        def b_left():
            got(1, slot(r1, 1))
            t[pl.ds(half, half), cols] = load(prv, 1) + val(r1, 1)
            go(5, slot(t, 1), slot(r2, 3), left)

        def c_():
            got(3, slot(r2, 2))
            got(4, slot(r2, 0))
            dst[pl.ds(0, half), cols] = load(p, 0) + (val(r2, 0) + val(r2, 2))
            got(2, slot(r2, 1))
            got(5, slot(r2, 3))
            dst[pl.ds(half, half), cols] = load(p, 1) + (val(r2, 1) + val(r2, 3))

        return a, b_right, b_left, c_

    def ag_stages(c, first, axis, p, piece):
        right, left = along(axis, 1), along(axis, -1)
        nxt, far, prv = lax.rem(p + 1, 4), lax.rem(p + 2, 4), lax.rem(p + 3, 4)

        def desc(k, ref, to):
            return pltpu.make_async_remote_copy(
                ref, ref, ssem.at[c, first + k], rsem.at[c, first + k],
                device_id=to, device_id_type=MESH)

        def go(k, ref, to):
            d = desc(k, ref, to)
            d.start()
            sends.append(d)

        def a():
            go(0, piece(p, None), right)
            go(1, piece(p, None), left)

        def b_right():
            desc(0, piece(prv, None), right).wait_recv()
            go(2, piece(prv, 0), right)

        def b_left():
            desc(1, piece(nxt, None), right).wait_recv()
            go(3, piece(nxt, 1), left)

        def c_():
            desc(2, piece(far, 0), right).wait_recv()
            desc(3, piece(far, 1), right).wait_recv()

        return a, b_right, b_left, c_

    big, mid, small = nt // 4, nt // 16, nt // 32

    def chunk(c, col, size, order):
        edge = order is None
        first = 1 if edge else order
        second = 1 - first
        pos = (x, y)
        p1, p2 = pos[first], pos[second]
        cols = pl.ds(col, size)

        def rows(q, h, unit, base=0):
            start = base + q * unit
            if h is None:
                return pl.ds(pl.multiple_of(start, unit), unit)
            return pl.ds(pl.multiple_of(start + h * (unit // 2), unit // 2), unit // 2)

        def src1(q, h):
            if edge:
                return edge_part, rows(q, h, big), pl.ds(0, size)
            return part, rows(q, h, big), cols

        def src2(q, h):
            return q1, rows(q, h, mid), cols

        a1, b1r, b1l, c1 = rs_stages(c, 0, first, p1, src1, cols, big // 2, r1, r2, t1, q1)
        a2, b2r, b2l, c2 = rs_stages(c, RS, second, p2, src2, cols, mid // 2, s1, s2, u1, q2)
        base = p1 * big

        def piece2(q, h):
            return full.at[rows(q, h, mid, base), cols]

        def piece1(q, h):
            return full.at[rows(q, h, big), cols]

        g2, h2r, h2l, i2 = ag_stages(c, 2 * RS + 1, second, p2, piece2)
        g1, h1r, h1l, i1 = ag_stages(c, 2 * RS + 1 + AG, first, p1, piece1)
        kz = 2 * RS
        swap = pltpu.make_async_remote_copy(
            q2.at[:, cols], zin.at[:, cols], ssem.at[c, kz], rsem.at[c, kz],
            device_id=across, device_id_type=MESH)

        def stage0():
            if edge:
                edges()
            a1()

        def stage2():
            c1()
            a2()

        def stage4():
            c2()
            swap.start()
            sends.append(swap)

        def stage5():
            swap.wait_recv()
            mine = pl.ds(pl.multiple_of(base + p2 * mid, mid), mid)
            full[mine, cols] = (q2[:, cols] + zin[:, cols]) * (1.0 / (ns * NZ * NX * NY))
            g2()

        def stage7():
            i2()
            g1()

        def stage9():
            i1()
            if edge:
                half = size // 2
                dst = [(col, 0, half), (col + half, own - half, half)]
            else:
                dst = [(col, col + width, size)]
            for k, (a, b, w) in enumerate(dst):
                d = pltpu.make_async_copy(
                    full.at[:, pl.ds(a, w)], out.at[:, pl.ds(b, w)], osem.at[c + k])
                d.start()
                outs.append(d)

        return (stage0, b1r, b1l, stage2, b2r, b2l, stage4, stage5, h2r, h2l, stage7, h1r, h1l, stage9)

    outs = []
    work = [chunk(c, *spec) for c, spec in enumerate(chunks)]
    for code in ORDER:
        work[code % len(work)][code // len(work)]()
    for d in sends:
        d.wait_send()
    pl.when(upper)(lambda: edge_sent(True))
    pl.when(lower)(lambda: edge_sent(False))
    for d in outs:
        d.wait()


def reduce(partial, sums, ns, width, n):
    nt, own = partial.shape
    count = len(WIDTHS)
    chunks = tuple(
        (sum(WIDTHS[:k]), WIDTHS[k], k % 2 if k < count - 1 else None) for k in range(count))

    def rows(k):
        return pltpu.VMEM((k, own), F32)

    sem = pltpu.SemaphoreType.DMA
    return pl.pallas_call(
        functools.partial(reduce_kernel, n, ns, chunks),
        out_shape=(
            jax.ShapeDtypeStruct((nt, own), F32),
            jax.ShapeDtypeStruct((2, ns, nt, width), BF16),
        ),
        in_specs=[VM] * 2,
        out_specs=(ANY, VM),
        scratch_shapes=[
            rows(nt),
            pltpu.VMEM((nt, 2 * width), F32),
            pltpu.VMEM((2, ns * nt + 8, width), F32),
            rows(nt // 4), rows(nt // 2), rows(nt // 4), rows(nt // 4),
            rows(nt // 16), rows(nt // 8), rows(nt // 16), rows(nt // 16), rows(nt // 16),
            sem((count, SENDS)), sem((count, SENDS)), sem((2, 2)), sem((count + 1,)),
        ],
        compiler_params=pltpu.CompilerParams(
            collective_id=1, has_side_effects=True, vmem_limit_bytes=20 << 20),
        name="reduce",
    )(partial, sums)


def finish_kernel(aligned_in, edge_aligned, template_in, aligned, template, sem):
    own = aligned.shape[2]
    width = edge_aligned.shape[3]
    stores = [pltpu.make_async_copy(template_in, template, sem.at[2])]
    for side in range(2):
        cols = pl.ds(0 if side == 0 else own - width, width)
        stores.append(pltpu.make_async_copy(
            edge_aligned.at[side], aligned.at[:, :, cols], sem.at[side]))
    for c in stores:
        c.start()
    for c in stores:
        c.wait()


def finish(aligned, edge_aligned, template):
    return pl.pallas_call(
        finish_kernel,
        out_shape=(
            jax.ShapeDtypeStruct(aligned.shape, aligned.dtype),
            jax.ShapeDtypeStruct(template.shape, template.dtype),
        ),
        in_specs=[HBM, VM, VM],
        out_specs=(HBM, HBM),
        scratch_shapes=[pltpu.SemaphoreType.DMA((3,))],
        input_output_aliases={0: 0},
        compiler_params=pltpu.CompilerParams(vmem_limit_bytes=8 << 20),
        name="finish",
    )(aligned, edge_aligned, template)


def local(n, data, template, centres, neighbours):
    width = neighbours.shape[1]
    wide = halos(data, template, n, width)
    aligned, partial, sums = align(centres, neighbours, wide, data.shape)
    new_template, edge_aligned = reduce(partial, sums, data.shape[0], width, n)
    return finish(aligned, edge_aligned, new_template)


def solution(mesh):
    in_specs = (P("subj", None, "vert"), P(None, "vert"), P("vert"), P("vert", None))
    out_specs = (P("subj", None, "vert"), P(None, "vert"))
    return jax.shard_map(
        functools.partial(local, mesh.shape["vert"]), mesh=mesh,
        in_specs=in_specs, out_specs=out_specs, check_vma=False)
```

```python
import functools

import jax
import jax.numpy as jnp
from jax import lax
from jax.experimental import pallas as pl
from jax.experimental.pallas import tpu as pltpu
from jax.sharding import PartitionSpec as P

NS_STEPS = 4
UNROLL = 4
MESH = pl.DeviceIdType.MESH
ANY = pl.BlockSpec(memory_space=pl.ANY)
VM = pl.BlockSpec(memory_space=pltpu.VMEM)
HBM = pl.BlockSpec(memory_space=pltpu.HBM)
SM = pl.BlockSpec(memory_space=pltpu.SMEM)
F32, BF16 = jnp.float32, jnp.bfloat16
LANES = 128


def dot(a, b, dims):
    return lax.dot_general(a, b, (dims, ((), ())), preferred_element_type=F32)


NN, NT, TN = ((1,), (0,)), ((1,), (1,)), ((0,), (0,))


def pieces(x):
    hi = x.astype(BF16)
    return hi, (x - hi.astype(F32)).astype(BF16)


def halo_kernel(n, data, tmpl, wide, lsem, ssem, rsem):
    v = lax.axis_index("vert")
    ns, nt, own = data.shape
    width = (wide.shape[1] - own) // 2
    barrier = pltpu.get_barrier_semaphore()
    lower, upper = v > 0, v < n - 1

    def greet(other):
        pl.semaphore_signal(barrier, inc=1, device_id={"vert": other}, device_id_type=MESH)

    def rows(i):
        return pl.ds(i * nt, nt)

    def src(i, cols):
        return data.at[i, :, cols] if i < ns else tmpl.at[:, cols]

    pl.when(lower)(lambda: greet(v - 1))
    pl.when(upper)(lambda: greet(v + 1))
    mine = [
        pltpu.make_async_copy(
            src(i, pl.ds(0, own)), wide.at[rows(i), pl.ds(width, own)], lsem.at[i])
        for i in range(ns + 1)
    ]
    for c in mine:
        c.start()
    pl.semaphore_wait(barrier, jnp.minimum(v, 1) + jnp.minimum(n - 1 - v, 1))

    def copies(up):
        cols = pl.ds(own - width, width) if up else pl.ds(0, width)
        dst = pl.ds(0, width) if up else pl.ds(width + own, width)
        to = {"vert": v + 1 if up else v - 1}
        k = 0 if up else ns + 1
        return [
            pltpu.make_async_remote_copy(
                src(i, cols), wide.at[rows(i), dst], ssem.at[k + i], rsem.at[k + i],
                device_id=to, device_id_type=MESH)
            for i in range(ns + 1)
        ]

    def start(up):
        for c in copies(up):
            c.start()

    def sent(up):
        for c in copies(up):
            c.wait_send()

    def received(up):
        for c in copies(up):
            c.wait_recv()

    def blank(at):
        wide[:, pl.ds(at, width)] = jnp.zeros((wide.shape[0], width), wide.dtype)

    pl.when(upper)(lambda: start(True))
    pl.when(lower)(lambda: start(False))
    pl.when(jnp.logical_not(lower))(lambda: blank(0))
    pl.when(jnp.logical_not(upper))(lambda: blank(width + own))
    for c in mine:
        c.wait()
    pl.when(upper)(lambda: sent(True))
    pl.when(lower)(lambda: sent(False))
    pl.when(lower)(lambda: received(True))
    pl.when(upper)(lambda: received(False))


def halos(data, template, n, width):
    ns, nt, own = data.shape
    sem = pltpu.SemaphoreType.DMA
    return pl.pallas_call(
        functools.partial(halo_kernel, n),
        out_shape=jax.ShapeDtypeStruct(((ns + 1) * nt, own + 2 * width), data.dtype),
        in_specs=[HBM, HBM],
        out_specs=VM,
        scratch_shapes=[sem((ns + 1,)), sem((2 * ns + 2,)), sem((2 * ns + 2,))],
        compiler_params=pltpu.CompilerParams(
            collective_id=0, has_side_effects=True, vmem_limit_bytes=8 << 20),
        name="halo",
    )(*(pltpu.with_memory_space_constraint(a, pltpu.HBM) for a in (data, template)))


def align_kernel(ns, unroll, cen, nb, wide, aligned, partial, acc, xbuf, zbuf, ybuf):
    lights, width = nb.shape
    nt, own = partial.shape
    tiles = own // LANES
    groups = lights // unroll
    lane = lax.broadcasted_iota(jnp.int32, (1, LANES), 1)

    def rows(i):
        return pl.ds(i * nt, nt)

    acc[...] = jnp.zeros_like(acc)
    ones = jnp.ones((16, width), BF16)
    none = jnp.zeros((16, width), BF16)

    def window(c):
        local = lax.rem(cen[c], own)
        base = pl.multiple_of(lax.div(local, LANES) * LANES, LANES)
        target = nb[pl.ds(c, 1), :] + width
        pick = (lax.broadcasted_iota(jnp.int32, (2 * LANES, width), 0) == target)
        return base, local - base, pick.astype(F32).astype(BF16)

    def gather(g):
        for u in range(unroll):
            base, off, pick = window(g * unroll + u)
            back = lax.rem(LANES - off, LANES)
            kept = lane < LANES - off
            x = []
            for i in range(ns + 1):
                p, q, r = (
                    pltpu.roll(wide[rows(i), pl.ds(base + k * LANES, LANES)], back, 1)
                    for k in range(3))
                seen = jnp.concatenate([jnp.where(kept, p, q), jnp.where(kept, q, r)], axis=1)
                x.append(dot(seen, pick, NN).astype(BF16))
                yield
            m = x.pop()
            for i in range(ns):
                xbuf[lax.rem(g, 3), u * ns + i] = x[i]
            both = dot(m, jnp.concatenate(x, axis=1), TN)
            for i in range(ns):
                z = both[:, i * width:(i + 1) * width]
                norm = jnp.sum(z * z, axis=(0, 1), keepdims=True)
                zbuf[lax.rem(g, 2), u * ns + i] = z * (1.0 / jnp.sqrt(norm + 1e-06))
            yield

    def iterate(g):
        zs = [zbuf[lax.rem(g, 2), k] for k in range(unroll * ns)]
        for step in range(NS_STEPS):
            grams = []
            for z in zs:
                zh, zl = pieces(z)
                a = jnp.concatenate([zh, zl], axis=1)
                b = jnp.concatenate(
                    [jnp.concatenate([zh, zh], axis=1), jnp.concatenate([zl, zl], axis=1)], axis=0)
                p = dot(a, b, NT)
                grams.append((p[:, :width] + p[:, width:], zh, zl))
                yield
            nxt = []
            for z, (gram, zh, zl) in zip(zs, grams):
                gh, gl = pieces(gram)
                a = jnp.concatenate([gh, gl], axis=1)
                b = jnp.concatenate([zh, zl], axis=1)
                p = dot(a, jnp.concatenate([b, b], axis=0), NN)
                nxt.append(1.5 * z - 0.5 * (p[:, :width] + p[:, width:]))
                yield
            zs = nxt
        for k, z in enumerate(zs):
            ybuf[lax.rem(g, 2), k] = jnp.concatenate(pieces(z), axis=1)

    def scatter(g):
        for u in range(unroll):
            base, off, pick = window(g * unroll + u)
            parts = []
            for i in range(ns):
                x = xbuf[lax.rem(g, 3), u * ns + i]
                turned = dot(
                    jnp.concatenate([x, x], axis=1), ybuf[lax.rem(g, 2), u * ns + i], NT)
                parts.append(jnp.concatenate(pieces(turned), axis=1))
                yield
            parts[-1] = jnp.concatenate([parts[-1], jnp.concatenate([ones, none], axis=1)], axis=0)
            twice = jnp.concatenate([pick, pick], axis=1)
            inside = lane >= off
            for i in range(ns):
                spread = dot(parts[i], twice, NT)
                at = pl.ds(i * nt, spread.shape[0])
                p, q = (pltpu.roll(spread[:, k * LANES:(k + 1) * LANES], off, 1) for k in range(2))
                acc[at, pl.ds(base, LANES)] += jnp.where(inside, p, 0.0)
                acc[at, pl.ds(base + LANES, LANES)] += jnp.where(inside, q, p)
                acc[at, pl.ds(base + 2 * LANES, LANES)] += jnp.where(inside, 0.0, q)
                yield

    def together(*works):
        works = [[w, n, 0] for w, n in works]
        while works:
            w = min(works, key=lambda w: (w[2] + 0.5) / w[1])
            w[2] += 1
            if next(w[0], works) is works:
                works.remove(w)

    def gathering(g):
        return gather(g), unroll * (ns + 2)

    def iterating(g):
        return iterate(g), 2 * NS_STEPS * unroll * ns

    def scattering(g):
        return scatter(g), unroll * 2 * ns

    def body(g, _):
        together(scattering(g - 1), iterating(g), gathering(g + 1))
        return 0

    together(gathering(0))
    together(iterating(0), gathering(1))
    lax.fori_loop(1, groups - 1, body, 0)
    together(scattering(groups - 2), iterating(groups - 1))
    together(scattering(groups - 1))
    for t in range(1, tiles - 1):
        src = pl.ds((t + 1) * LANES, LANES)
        dst = pl.ds(t * LANES, LANES)
        inv = 1.0 / jnp.maximum(acc[pl.ds(ns * nt, 1), src], 1.0)
        total = None
        for i in range(ns):
            mapped = acc[rows(i), src] * inv
            aligned[i, :, dst] = mapped.astype(BF16)
            total = mapped if total is None else total + mapped
        partial[:, pl.ds((t - 1) * LANES, LANES)] = total


def align(centres, neighbours, wide, shape):
    ns, nt, own = shape
    width = neighbours.shape[1]
    return pl.pallas_call(
        functools.partial(align_kernel, ns, UNROLL),
        out_shape=(
            jax.ShapeDtypeStruct(shape, BF16),
            jax.ShapeDtypeStruct((nt, own), F32),
            jax.ShapeDtypeStruct((ns * nt + 16, wide.shape[1]), F32),
        ),
        in_specs=[SM, VM, VM],
        out_specs=(VM,) * 3,
        scratch_shapes=[
            pltpu.VMEM((3, UNROLL * ns, nt, width), BF16),
            pltpu.VMEM((2, UNROLL * ns, width, width), F32),
            pltpu.VMEM((2, UNROLL * ns, width, 2 * width), BF16),
        ],
        compiler_params=pltpu.CompilerParams(vmem_limit_bytes=24 << 20),
        name="align",
    )(centres, neighbours, wide)


NZ, NX, NY = 2, 4, 4
WIDTHS = (256, 256, 256, 256, 256, 256, 256, 256)
ORDER = (
    0, 1, 2, 3, 4, 5, 8, 9, 6, 7, 10, 11, 12, 13, 17, 16,
    14, 15, 19, 18, 21, 20, 25, 24, 22, 23, 33, 27, 32, 26, 29, 28,
    30, 31, 35, 41, 40, 34, 36, 37, 38, 39, 43, 42, 45, 44, 47, 46,
)
SENDS = 13


def reduce_kernel(n, ns, chunks, part, sums, out, edge_aligned, full, edge_part, edge_in,
                  r1, q1, r2, q2, zin,
                  ssem, rsem, esem, osem):
    s, v = lax.axis_index("subj"), lax.axis_index("vert")
    nt, own = full.shape
    width = edge_in.shape[2]
    y, x, zh = lax.rem(s, NY), lax.rem(lax.div(s, NY), NX), lax.div(s, NX * NY)

    def place(zh, x, y):
        return {"subj": (zh * NX + x) * NY + y}

    def along(axis, by):
        if axis == 0:
            return place(zh, lax.rem(x + by + NX, NX), y)
        return place(zh, x, lax.rem(y + by + NY, NY))

    across = place(NZ - 1 - zh, x, y)
    barrier = pltpu.get_barrier_semaphore()
    lower, upper = v > 0, v < n - 1

    def greet(to):
        pl.semaphore_signal(barrier, inc=1, device_id=to, device_id_type=MESH)

    for to in [along(axis, by) for axis in range(2) for by in (1, 2, -1)] + [across]:
        greet(to)
    pl.when(lower)(lambda: greet({"vert": v - 1}))
    pl.when(upper)(lambda: greet({"vert": v + 1}))
    pl.semaphore_wait(barrier, 7 + jnp.minimum(v, 1) + jnp.minimum(n - 1 - v, 1))

    def edge_copy(up):
        k = 1 if up else 0
        cols = pl.ds(width + own, width) if up else pl.ds(0, width)
        return pltpu.make_async_remote_copy(
            sums.at[pl.ds(0, ns * nt + 8), cols], edge_in.at[k], esem.at[0, k], esem.at[1, k],
            device_id={"vert": v + 1 if up else v - 1}, device_id_type=MESH)

    def edge_start(up):
        edge_copy(up).start()

    def edge_sent(up):
        edge_copy(up).wait_send()

    def edge_got(up):
        edge_copy(up).wait_recv()

    def edge_blank(up):
        k = 1 if up else 0
        edge_in[k] = jnp.zeros(edge_in.shape[1:], F32)

    pl.when(upper)(lambda: edge_start(True))
    pl.when(lower)(lambda: edge_start(False))
    pl.when(jnp.logical_not(lower))(lambda: edge_blank(True))
    pl.when(jnp.logical_not(upper))(lambda: edge_blank(False))

    def edges():
        pl.when(lower)(lambda: edge_got(True))
        pl.when(upper)(lambda: edge_got(False))
        for side in range(2):
            k = 1 - side
            at = pl.ds(width if side == 0 else own, width)
            count = sums[pl.ds(ns * nt, 1), at] + edge_in[k, pl.ds(ns * nt, 1), :]
            inv = 1.0 / jnp.maximum(count, 1.0)
            total = None
            for i in range(ns):
                mine = pl.ds(i * nt, nt)
                mapped = (sums[mine, at] + edge_in[k, mine, :]) * inv
                edge_aligned[side, i] = mapped.astype(BF16)
                total = mapped if total is None else total + mapped
            edge_part[:, side * width:(side + 1) * width] = total

    sends = []

    def remote(c, k, a, b, to):
        return pltpu.make_async_remote_copy(
            a, b, ssem.at[c, k], rsem.at[c, k], device_id=to, device_id_type=MESH)

    def go(*what):
        d = remote(*what)
        d.start()
        sends.append(d)

    hops = (2, 1, -1)

    def rs_stages(c, first, axis, p, src, cols, unit, r, dst):
        def slot(k):
            return pl.ds(k * unit, unit)

        def start():
            for k, by in enumerate(hops):
                ref, at, cc = src(lax.rem(p + by + 4, 4))
                go(c, first + k, ref.at[at, cc], r.at[slot(k), cols], along(axis, by))

        def end():
            for k in (1, 2, 0):
                b = r.at[slot(k), cols]
                remote(c, first + k, b, b, along(axis, 1)).wait_recv()
            ref, at, cc = src(p)
            dst[:, cols] = (ref[at, cc] + r[slot(0), cols]) + (r[slot(1), cols] + r[slot(2), cols])

        return start, end

    def ag_stages(c, first, axis, p, piece):
        def start():
            for k, by in enumerate(hops):
                go(c, first + k, piece(p), piece(p), along(axis, by))

        def end():
            for k, by in enumerate(hops):
                b = piece(lax.rem(p - by + 4, 4))
                remote(c, first + k, b, b, along(axis, 1)).wait_recv()

        return start, end

    big, mid = nt // 4, nt // 16

    def chunk(c, col, size, order):
        edge = order is None
        first = 1 if edge else order
        second = 1 - first
        pos = (x, y)
        p1, p2 = pos[first], pos[second]
        cols = pl.ds(col, size)

        def rows(q, unit, base=0):
            return pl.ds(pl.multiple_of(base + q * unit, unit), unit)

        def src1(q):
            if edge:
                return edge_part, rows(q, big), pl.ds(0, size)
            return part, rows(q, big), cols

        def src2(q):
            return q1, rows(q, mid), cols

        a1, c1 = rs_stages(c, 0, first, p1, src1, cols, big, r1, q1)
        a2, c2 = rs_stages(c, 3, second, p2, src2, cols, mid, r2, q2)
        base = p1 * big
        g2, i2 = ag_stages(c, 7, second, p2, lambda q: full.at[rows(q, mid, base), cols])
        g1, i1 = ag_stages(c, 10, first, p1, lambda q: full.at[rows(q, big), cols])
        z = c, 6, q2.at[:, cols], zin.at[:, cols], across

        def stage0():
            if edge:
                edges()
            a1()

        def stage1():
            c1()
            a2()

        def stage2():
            c2()
            go(*z)

        def stage3():
            remote(*z).wait_recv()
            full[rows(p2, mid, base), cols] = (q2[:, cols] + zin[:, cols]) * (
                1.0 / (ns * NZ * NX * NY))
            g2()

        def stage4():
            i2()
            g1()

        def stage5():
            i1()
            if edge:
                half = size // 2
                dst = [(col, 0, half), (col + half, own - half, half)]
            else:
                dst = [(col, col + width, size)]
            for k, (a, b, w) in enumerate(dst):
                d = pltpu.make_async_copy(
                    full.at[:, pl.ds(a, w)], out.at[:, pl.ds(b, w)], osem.at[c + k])
                d.start()
                outs.append(d)

        return stage0, stage1, stage2, stage3, stage4, stage5

    outs = []
    work = [chunk(c, *spec) for c, spec in enumerate(chunks)]
    for code in ORDER:
        work[code % len(work)][code // len(work)]()
    for d in sends:
        d.wait_send()
    pl.when(upper)(lambda: edge_sent(True))
    pl.when(lower)(lambda: edge_sent(False))
    for d in outs:
        d.wait()


def reduce(partial, sums, ns, width, n):
    nt, own = partial.shape
    count = len(WIDTHS)
    chunks = tuple(
        (sum(WIDTHS[:k]), WIDTHS[k], k % 2 if k < count - 1 else None) for k in range(count))

    def rows(k):
        return pltpu.VMEM((k, own), F32)

    sem = pltpu.SemaphoreType.DMA
    return pl.pallas_call(
        functools.partial(reduce_kernel, n, ns, chunks),
        out_shape=(
            jax.ShapeDtypeStruct((nt, own), F32),
            jax.ShapeDtypeStruct((2, ns, nt, width), BF16),
        ),
        in_specs=[VM] * 2,
        out_specs=(ANY, VM),
        scratch_shapes=[
            rows(nt),
            pltpu.VMEM((nt, 2 * width), F32),
            pltpu.VMEM((2, ns * nt + 8, width), F32),
            rows(3 * nt // 4), rows(nt // 4), rows(3 * nt // 16), rows(nt // 16), rows(nt // 16),
            sem((count, SENDS)), sem((count, SENDS)), sem((2, 2)), sem((count + 1,)),
        ],
        compiler_params=pltpu.CompilerParams(
            collective_id=1, has_side_effects=True, vmem_limit_bytes=20 << 20),
        name="reduce",
    )(partial, sums)


def finish_kernel(aligned_in, edge_aligned, template_in, aligned, template, sem):
    own = aligned.shape[2]
    width = edge_aligned.shape[3]
    stores = [pltpu.make_async_copy(template_in, template, sem.at[2])]
    for side in range(2):
        cols = pl.ds(0 if side == 0 else own - width, width)
        stores.append(pltpu.make_async_copy(
            edge_aligned.at[side], aligned.at[:, :, cols], sem.at[side]))
    for c in stores:
        c.start()
    for c in stores:
        c.wait()


def finish(aligned, edge_aligned, template):
    return pl.pallas_call(
        finish_kernel,
        out_shape=(
            jax.ShapeDtypeStruct(aligned.shape, aligned.dtype),
            jax.ShapeDtypeStruct(template.shape, template.dtype),
        ),
        in_specs=[HBM, VM, VM],
        out_specs=(HBM, HBM),
        scratch_shapes=[pltpu.SemaphoreType.DMA((3,))],
        input_output_aliases={0: 0},
        compiler_params=pltpu.CompilerParams(vmem_limit_bytes=8 << 20),
        name="finish",
    )(aligned, edge_aligned, template)


def local(n, data, template, centres, neighbours):
    width = neighbours.shape[1]
    wide = halos(data, template, n, width)
    aligned, partial, sums = align(centres, neighbours, wide, data.shape)
    new_template, edge_aligned = reduce(partial, sums, data.shape[0], width, n)
    return finish(aligned, edge_aligned, new_template)


def solution(mesh):
    in_specs = (P("subj", None, "vert"), P(None, "vert"), P("vert"), P("vert", None))
    out_specs = (P("subj", None, "vert"), P(None, "vert"))
    return jax.shard_map(
        functools.partial(local, mesh.shape["vert"]), mesh=mesh,
        in_specs=in_specs, out_specs=out_specs, check_vma=False)
```

```python
import functools

import jax
import jax.numpy as jnp
from jax import lax
from jax.experimental import pallas as pl
from jax.experimental.pallas import tpu as pltpu
from jax.sharding import PartitionSpec as P

NS_STEPS = 4
UNROLL = 4
MESH = pl.DeviceIdType.MESH
ANY = pl.BlockSpec(memory_space=pl.ANY)
VM = pl.BlockSpec(memory_space=pltpu.VMEM)
HBM = pl.BlockSpec(memory_space=pltpu.HBM)
SM = pl.BlockSpec(memory_space=pltpu.SMEM)
F32, BF16 = jnp.float32, jnp.bfloat16
LANES = 128


def dot(a, b, dims):
    return lax.dot_general(a, b, (dims, ((), ())), preferred_element_type=F32)


NN, NT, TN = ((1,), (0,)), ((1,), (1,)), ((0,), (0,))


def pieces(x):
    hi = x.astype(BF16)
    return hi, (x - hi.astype(F32)).astype(BF16)


def halo_kernel(n, data, tmpl, wide, lsem, ssem, rsem):
    v = lax.axis_index("vert")
    ns, nt, own = data.shape
    width = (wide.shape[1] - own) // 2
    barrier = pltpu.get_barrier_semaphore()
    lower, upper = v > 0, v < n - 1

    def greet(other):
        pl.semaphore_signal(barrier, inc=1, device_id={"vert": other}, device_id_type=MESH)

    def rows(i):
        return pl.ds(i * nt, nt)

    def src(i, cols):
        return data.at[i, :, cols] if i < ns else tmpl.at[:, cols]

    pl.when(lower)(lambda: greet(v - 1))
    pl.when(upper)(lambda: greet(v + 1))
    mine = [
        pltpu.make_async_copy(
            src(i, pl.ds(0, own)), wide.at[rows(i), pl.ds(width, own)], lsem.at[i])
        for i in range(ns + 1)
    ]
    for c in mine:
        c.start()
    pl.semaphore_wait(barrier, jnp.minimum(v, 1) + jnp.minimum(n - 1 - v, 1))

    def copies(up):
        cols = pl.ds(own - width, width) if up else pl.ds(0, width)
        dst = pl.ds(0, width) if up else pl.ds(width + own, width)
        to = {"vert": v + 1 if up else v - 1}
        k = 0 if up else ns + 1
        return [
            pltpu.make_async_remote_copy(
                src(i, cols), wide.at[rows(i), dst], ssem.at[k + i], rsem.at[k + i],
                device_id=to, device_id_type=MESH)
            for i in range(ns + 1)
        ]

    def start(up):
        for c in copies(up):
            c.start()

    def sent(up):
        for c in copies(up):
            c.wait_send()

    def received(up):
        for c in copies(up):
            c.wait_recv()

    def blank(at):
        wide[:, pl.ds(at, width)] = jnp.zeros((wide.shape[0], width), wide.dtype)

    pl.when(upper)(lambda: start(True))
    pl.when(lower)(lambda: start(False))
    pl.when(jnp.logical_not(lower))(lambda: blank(0))
    pl.when(jnp.logical_not(upper))(lambda: blank(width + own))
    for c in mine:
        c.wait()
    pl.when(upper)(lambda: sent(True))
    pl.when(lower)(lambda: sent(False))
    pl.when(lower)(lambda: received(True))
    pl.when(upper)(lambda: received(False))


def halos(data, template, n, width):
    ns, nt, own = data.shape
    sem = pltpu.SemaphoreType.DMA
    return pl.pallas_call(
        functools.partial(halo_kernel, n),
        out_shape=jax.ShapeDtypeStruct(((ns + 1) * nt, own + 2 * width), data.dtype),
        in_specs=[HBM, HBM],
        out_specs=VM,
        scratch_shapes=[sem((ns + 1,)), sem((2 * ns + 2,)), sem((2 * ns + 2,))],
        compiler_params=pltpu.CompilerParams(
            collective_id=0, has_side_effects=True, vmem_limit_bytes=8 << 20),
        name="halo",
    )(*(pltpu.with_memory_space_constraint(a, pltpu.HBM) for a in (data, template)))


def align_kernel(ns, unroll, cen, nb, wide, aligned, partial, acc, xbuf, zbuf, ybuf):
    lights, width = nb.shape
    nt, own = partial.shape
    tiles = own // LANES
    groups = lights // unroll
    lane = lax.broadcasted_iota(jnp.int32, (1, LANES), 1)

    def rows(i):
        return pl.ds(i * nt, nt)

    acc[...] = jnp.zeros_like(acc)
    ones = jnp.ones((16, width), BF16)
    none = jnp.zeros((16, width), BF16)

    def window(c):
        local = lax.rem(cen[c], own)
        base = pl.multiple_of(lax.div(local, LANES) * LANES, LANES)
        target = nb[pl.ds(c, 1), :] + width
        pick = (lax.broadcasted_iota(jnp.int32, (2 * LANES, width), 0) == target)
        return base, local - base, pick.astype(F32).astype(BF16)

    def gather(g):
        for u in range(unroll):
            base, off, pick = window(g * unroll + u)
            back = lax.rem(LANES - off, LANES)
            kept = lane < LANES - off
            x = []
            for i in range(ns + 1):
                p, q, r = (
                    pltpu.roll(wide[rows(i), pl.ds(base + k * LANES, LANES)], back, 1)
                    for k in range(3))
                seen = jnp.concatenate([jnp.where(kept, p, q), jnp.where(kept, q, r)], axis=1)
                x.append(dot(seen, pick, NN).astype(BF16))
                yield
            m = x.pop()
            for i in range(ns):
                xbuf[lax.rem(g, 3), u * ns + i] = x[i]
            both = dot(m, jnp.concatenate(x, axis=1), TN)
            for i in range(ns):
                z = both[:, i * width:(i + 1) * width]
                norm = jnp.sum(z * z, axis=(0, 1), keepdims=True)
                zbuf[lax.rem(g, 2), u * ns + i] = z * (1.0 / jnp.sqrt(norm + 1e-06))
            yield

    def iterate(g):
        zs = [zbuf[lax.rem(g, 2), k] for k in range(unroll * ns)]
        for step in range(NS_STEPS):
            grams = []
            for z in zs:
                zh, zl = pieces(z)
                a = jnp.concatenate([zh, zl], axis=1)
                b = jnp.concatenate(
                    [jnp.concatenate([zh, zh], axis=1), jnp.concatenate([zl, zl], axis=1)], axis=0)
                p = dot(a, b, NT)
                grams.append((p[:, :width] + p[:, width:], zh, zl))
                yield
            nxt = []
            for z, (gram, zh, zl) in zip(zs, grams):
                gh, gl = pieces(gram)
                a = jnp.concatenate([gh, gl], axis=1)
                b = jnp.concatenate([zh, zl], axis=1)
                p = dot(a, jnp.concatenate([b, b], axis=0), NN)
                nxt.append(1.5 * z - 0.5 * (p[:, :width] + p[:, width:]))
                yield
            zs = nxt
        for k, z in enumerate(zs):
            ybuf[lax.rem(g, 2), k] = jnp.concatenate(pieces(z), axis=1)

    def scatter(g):
        for u in range(unroll):
            base, off, pick = window(g * unroll + u)
            parts = []
            for i in range(ns):
                x = xbuf[lax.rem(g, 3), u * ns + i]
                turned = dot(
                    jnp.concatenate([x, x], axis=1), ybuf[lax.rem(g, 2), u * ns + i], NT)
                parts.append(jnp.concatenate(pieces(turned), axis=1))
                yield
            parts[-1] = jnp.concatenate([parts[-1], jnp.concatenate([ones, none], axis=1)], axis=0)
            twice = jnp.concatenate([pick, pick], axis=1)
            inside = lane >= off
            for i in range(ns):
                spread = dot(parts[i], twice, NT)
                at = pl.ds(i * nt, spread.shape[0])
                p, q = (pltpu.roll(spread[:, k * LANES:(k + 1) * LANES], off, 1) for k in range(2))
                acc[at, pl.ds(base, LANES)] += jnp.where(inside, p, 0.0)
                acc[at, pl.ds(base + LANES, LANES)] += jnp.where(inside, q, p)
                acc[at, pl.ds(base + 2 * LANES, LANES)] += jnp.where(inside, 0.0, q)
                yield

    def together(*works):
        works = [[w, n, 0] for w, n in works]
        while works:
            w = min(works, key=lambda w: (w[2] + 0.5) / w[1])
            w[2] += 1
            if next(w[0], works) is works:
                works.remove(w)

    def gathering(g):
        return gather(g), unroll * (ns + 2)

    def iterating(g):
        return iterate(g), 2 * NS_STEPS * unroll * ns

    def scattering(g):
        return scatter(g), unroll * 2 * ns

    def body(g, _):
        together(scattering(g - 1), iterating(g), gathering(g + 1))
        return 0

    together(gathering(0))
    together(iterating(0), gathering(1))
    lax.fori_loop(1, groups - 1, body, 0)
    together(scattering(groups - 2), iterating(groups - 1))
    together(scattering(groups - 1))
    for t in range(1, tiles - 1):
        src = pl.ds((t + 1) * LANES, LANES)
        dst = pl.ds(t * LANES, LANES)
        inv = 1.0 / jnp.maximum(acc[pl.ds(ns * nt, 1), src], 1.0)
        total = None
        for i in range(ns):
            mapped = acc[rows(i), src] * inv
            aligned[i, :, dst] = mapped.astype(BF16)
            total = mapped if total is None else total + mapped
        partial[:, pl.ds((t - 1) * LANES, LANES)] = total


def align(centres, neighbours, wide, shape):
    ns, nt, own = shape
    width = neighbours.shape[1]
    return pl.pallas_call(
        functools.partial(align_kernel, ns, UNROLL),
        out_shape=(
            jax.ShapeDtypeStruct(shape, BF16),
            jax.ShapeDtypeStruct((nt, own), F32),
            jax.ShapeDtypeStruct((ns * nt + 16, wide.shape[1]), F32),
        ),
        in_specs=[SM, VM, VM],
        out_specs=(VM,) * 3,
        scratch_shapes=[
            pltpu.VMEM((3, UNROLL * ns, nt, width), BF16),
            pltpu.VMEM((2, UNROLL * ns, width, width), F32),
            pltpu.VMEM((2, UNROLL * ns, width, 2 * width), BF16),
        ],
        compiler_params=pltpu.CompilerParams(vmem_limit_bytes=24 << 20),
        name="align",
    )(centres, neighbours, wide)


NZ, NX, NY = 2, 4, 4
WIDTHS = (256, 256, 256, 256, 256, 256, 256, 256)
ORDER = (
    0, 1, 2, 3, 4, 5, 6, 7, 8, 9, 10, 11, 12, 13, 14, 15,
    17, 16, 18, 19, 20, 21, 22, 23, 25, 24, 26, 27, 28, 29, 30, 31,
    33, 32, 34, 35, 36, 37, 38, 39, 41, 40, 43, 42, 45, 44, 47, 46,
)
SENDS = 13


def reduce_kernel(n, ns, chunks, part, sums, out, edge_aligned, full, edge_part, edge_in,
                  done, tx, rx, ag, q1, r2, q2, zin,
                  ssem, rsem, esem, osem):
    s, v = lax.axis_index("subj"), lax.axis_index("vert")
    nt, own = full.shape
    width = edge_in.shape[2]
    y, x, zh = lax.rem(s, NY), lax.rem(lax.div(s, NY), NX), lax.div(s, NX * NY)

    def place(zh, x, y):
        return {"subj": (zh * NX + x) * NY + y}

    def along(axis, by):
        if axis == 0:
            return place(zh, lax.rem(x + by + NX, NX), y)
        return place(zh, x, lax.rem(y + by + NY, NY))

    across = place(NZ - 1 - zh, x, y)
    barrier = pltpu.get_barrier_semaphore()
    lower, upper = v > 0, v < n - 1

    def greet(to):
        pl.semaphore_signal(barrier, inc=1, device_id=to, device_id_type=MESH)

    for to in [along(axis, by) for axis in range(2) for by in (1, 2, -1)] + [across]:
        greet(to)
    pl.when(lower)(lambda: greet({"vert": v - 1}))
    pl.when(upper)(lambda: greet({"vert": v + 1}))
    pl.semaphore_wait(barrier, 7 + jnp.minimum(v, 1) + jnp.minimum(n - 1 - v, 1))

    def edge_copy(up):
        k = 1 if up else 0
        cols = pl.ds(width + own, width) if up else pl.ds(0, width)
        return pltpu.make_async_remote_copy(
            sums.at[pl.ds(0, ns * nt + 8), cols], edge_in.at[k], esem.at[0, k], esem.at[1, k],
            device_id={"vert": v + 1 if up else v - 1}, device_id_type=MESH)

    def edge_start(up):
        edge_copy(up).start()

    def edge_sent(up):
        edge_copy(up).wait_send()

    def edge_got(up):
        edge_copy(up).wait_recv()

    def edge_blank(up):
        k = 1 if up else 0
        edge_in[k] = jnp.zeros(edge_in.shape[1:], F32)

    pl.when(upper)(lambda: edge_start(True))
    pl.when(lower)(lambda: edge_start(False))
    pl.when(jnp.logical_not(lower))(lambda: edge_blank(True))
    pl.when(jnp.logical_not(upper))(lambda: edge_blank(False))

    def edges():
        pl.when(lower)(lambda: edge_got(True))
        pl.when(upper)(lambda: edge_got(False))
        for side in range(2):
            k = 1 - side
            at = pl.ds(width if side == 0 else own, width)
            count = sums[pl.ds(ns * nt, 1), at] + edge_in[k, pl.ds(ns * nt, 1), :]
            inv = 1.0 / jnp.maximum(count, 1.0)
            total = None
            for i in range(ns):
                mine = pl.ds(i * nt, nt)
                mapped = (sums[mine, at] + edge_in[k, mine, :]) * inv
                edge_aligned[side, i] = mapped.astype(BF16)
                total = mapped if total is None else total + mapped
            edge_part[:, side * width:(side + 1) * width] = total

    sends = []

    def remote(c, k, a, b, to):
        return pltpu.make_async_remote_copy(
            a, b, ssem.at[c, k], rsem.at[c, k], device_id=to, device_id_type=MESH)

    def go(*what):
        d = remote(*what)
        d.start()
        sends.append(d)

    hops = (2, 1, -1)
    tall = 16
    big, mid = nt // 4, nt // 16

    def spots(unit, size):
        return [
            (slice(i, i + tall), slice(j, j + LANES))
            for i in range(0, unit, tall) for j in range(0, size, LANES)]

    def encode(x, ref, index):
        parts = [x[i, j] for i, j in spots(*x.shape)]
        peak = functools.reduce(jnp.maximum, [jnp.abs(t) for t in parts])
        power = jnp.ceil(jnp.log2(jnp.maximum(peak, 1e-30)))
        scale = jnp.exp2(15.0 - power)
        for k, t in enumerate(parts):
            code = jnp.clip(jnp.round(t * scale), -32767.0, 32767.0)
            ref[(*index, k)] = code.astype(jnp.int32).astype(jnp.int16)
        ref[(*index, len(parts))] = power.astype(jnp.int32).astype(jnp.int16)

    def decode(ref, index, count):
        power = ref[(*index, count)].astype(jnp.int32).astype(F32)
        scale = jnp.exp2(power - 15.0)
        return [ref[(*index, k)].astype(jnp.int32).astype(F32) * scale for k in range(count)]

    def rs_stages(c, first, axis, p, src, cols, unit, r, dst):
        def slot(k):
            return pl.ds(k * unit, unit)

        def start():
            for k, by in enumerate(hops):
                ref, at, cc = src(lax.rem(p + by + 4, 4))
                go(c, first + k, ref.at[at, cc], r.at[slot(k), cols], along(axis, by))

        def end():
            for k in (1, 2, 0):
                b = r.at[slot(k), cols]
                remote(c, first + k, b, b, along(axis, 1)).wait_recv()
            ref, at, cc = src(p)
            dst[:, cols] = (ref[at, cc] + r[slot(0), cols]) + (r[slot(1), cols] + r[slot(2), cols])

        return start, end

    def ag_stages(c, first, axis, p, piece):
        def start():
            for k, by in enumerate(hops):
                go(c, first + k, piece(p), piece(p), along(axis, by))

        def end():
            for k, by in enumerate(hops):
                b = piece(lax.rem(p - by + 4, 4))
                remote(c, first + k, b, b, along(axis, 1)).wait_recv()

        return start, end

    def coded_rs(c, axis, p, src, col, size):
        places = spots(big, size)

        def start():
            for k, by in enumerate(hops):
                ref, at, cc = src(lax.rem(p + by + 4, 4))
                encode(ref[at, cc], tx, (c, k))
                go(c, k, tx.at[c, k], rx.at[c, k], along(axis, by))

        def end():
            for k in (1, 2, 0):
                remote(c, k, rx.at[c, k], rx.at[c, k], along(axis, 1)).wait_recv()
            far, one, two = (decode(rx, (c, k), len(places)) for k in range(3))
            ref, at, cc = src(p)
            mine = ref[at, cc]
            for (i, j), f, a, b in zip(places, far, one, two):
                q1[i, col + j.start:col + j.stop] = (mine[i, j] + f) + (a + b)

        return start, end

    def coded_ag(c, axis, p, col, size):
        places = spots(big, size)

        def start():
            encode(full[pl.ds(pl.multiple_of(p * big, big), big), pl.ds(col, size)], ag, (c, p))
            for k, by in enumerate(hops):
                go(c, 10 + k, ag.at[c, p], ag.at[c, p], along(axis, by))

        def end():
            for k, by in enumerate(hops):
                b = ag.at[c, lax.rem(p - by + 4, 4)]
                remote(c, 10 + k, b, b, along(axis, 1)).wait_recv()
            for q in range(4):
                for (i, j), t in zip(places, decode(ag, (c, q), len(places))):
                    done[q * big + i.start:q * big + i.stop, col + j.start:col + j.stop] = t

        return start, end


    def chunk(c, col, size, order):
        edge = order is None
        first = 1 if edge else order
        second = 1 - first
        pos = (x, y)
        p1, p2 = pos[first], pos[second]
        cols = pl.ds(col, size)

        def rows(q, unit, base=0):
            return pl.ds(pl.multiple_of(base + q * unit, unit), unit)

        def src1(q):
            if edge:
                return edge_part, rows(q, big), pl.ds(0, size)
            return part, rows(q, big), cols

        def src2(q):
            return q1, rows(q, mid), cols

        a1, c1 = coded_rs(c, first, p1, src1, col, size)
        a2, c2 = rs_stages(c, 3, second, p2, src2, cols, mid, r2, q2)
        base = p1 * big
        g2, i2 = ag_stages(c, 7, second, p2, lambda q: full.at[rows(q, mid, base), cols])
        g1, i1 = coded_ag(c, first, p1, col, size)
        z = c, 6, q2.at[:, cols], zin.at[:, cols], across

        def stage0():
            if edge:
                edges()
            a1()

        def stage1():
            c1()
            a2()

        def stage2():
            c2()
            go(*z)

        def stage3():
            remote(*z).wait_recv()
            full[rows(p2, mid, base), cols] = (q2[:, cols] + zin[:, cols]) * (
                1.0 / (ns * NZ * NX * NY))
            g2()

        def stage4():
            i2()
            g1()

        def stage5():
            i1()
            if edge:
                half = size // 2
                dst = [(col, 0, half), (col + half, own - half, half)]
            else:
                dst = [(col, col + width, size)]
            for k, (a, b, w) in enumerate(dst):
                d = pltpu.make_async_copy(
                    done.at[:, pl.ds(a, w)], out.at[:, pl.ds(b, w)], osem.at[c + k])
                d.start()
                outs.append(d)

        return stage0, stage1, stage2, stage3, stage4, stage5

    outs = []
    work = [chunk(c, *spec) for c, spec in enumerate(chunks)]
    for code in ORDER:
        work[code % len(work)][code // len(work)]()
    for d in sends:
        d.wait_send()
    pl.when(upper)(lambda: edge_sent(True))
    pl.when(lower)(lambda: edge_sent(False))
    for d in outs:
        d.wait()


def reduce(partial, sums, ns, width, n):
    nt, own = partial.shape
    count = len(WIDTHS)
    chunks = tuple(
        (sum(WIDTHS[:k]), WIDTHS[k], k % 2 if k < count - 1 else None) for k in range(count))

    def rows(k):
        return pltpu.VMEM((k, own), F32)

    tiles = (nt // 4) * max(WIDTHS) // (16 * LANES) + 1

    def codes(k):
        return pltpu.VMEM((count, k, tiles, 16, LANES), jnp.int16)

    sem = pltpu.SemaphoreType.DMA
    return pl.pallas_call(
        functools.partial(reduce_kernel, n, ns, chunks),
        out_shape=(
            jax.ShapeDtypeStruct((nt, own), F32),
            jax.ShapeDtypeStruct((2, ns, nt, width), BF16),
        ),
        in_specs=[VM] * 2,
        out_specs=(ANY, VM),
        scratch_shapes=[
            rows(nt),
            pltpu.VMEM((nt, 2 * width), F32),
            pltpu.VMEM((2, ns * nt + 8, width), F32),
            rows(nt), codes(3), codes(3), codes(4),
            rows(nt // 4), rows(3 * nt // 16), rows(nt // 16), rows(nt // 16),
            sem((count, SENDS)), sem((count, SENDS)), sem((2, 2)), sem((count + 1,)),
        ],
        compiler_params=pltpu.CompilerParams(
            collective_id=1, has_side_effects=True, vmem_limit_bytes=28 << 20),
        name="reduce",
    )(partial, sums)


def finish_kernel(aligned_in, edge_aligned, template_in, aligned, template, sem):
    own = aligned.shape[2]
    width = edge_aligned.shape[3]
    stores = [pltpu.make_async_copy(template_in, template, sem.at[2])]
    for side in range(2):
        cols = pl.ds(0 if side == 0 else own - width, width)
        stores.append(pltpu.make_async_copy(
            edge_aligned.at[side], aligned.at[:, :, cols], sem.at[side]))
    for c in stores:
        c.start()
    for c in stores:
        c.wait()


def finish(aligned, edge_aligned, template):
    return pl.pallas_call(
        finish_kernel,
        out_shape=(
            jax.ShapeDtypeStruct(aligned.shape, aligned.dtype),
            jax.ShapeDtypeStruct(template.shape, template.dtype),
        ),
        in_specs=[HBM, VM, VM],
        out_specs=(HBM, HBM),
        scratch_shapes=[pltpu.SemaphoreType.DMA((3,))],
        input_output_aliases={0: 0},
        compiler_params=pltpu.CompilerParams(vmem_limit_bytes=8 << 20),
        name="finish",
    )(aligned, edge_aligned, template)


def local(n, data, template, centres, neighbours):
    width = neighbours.shape[1]
    wide = halos(data, template, n, width)
    aligned, partial, sums = align(centres, neighbours, wide, data.shape)
    new_template, edge_aligned = reduce(partial, sums, data.shape[0], width, n)
    return finish(aligned, edge_aligned, new_template)


def solution(mesh):
    in_specs = (P("subj", None, "vert"), P(None, "vert"), P("vert"), P("vert", None))
    out_specs = (P("subj", None, "vert"), P(None, "vert"))
    return jax.shard_map(
        functools.partial(local, mesh.shape["vert"]), mesh=mesh,
        in_specs=in_specs, out_specs=out_specs, check_vma=False)
```

```python
import functools

import jax
import jax.numpy as jnp
from jax import lax
from jax.experimental import pallas as pl
from jax.experimental.pallas import tpu as pltpu
from jax.sharding import PartitionSpec as P

NS_STEPS = 4
UNROLL = 4
MESH = pl.DeviceIdType.MESH
ANY = pl.BlockSpec(memory_space=pl.ANY)
VM = pl.BlockSpec(memory_space=pltpu.VMEM)
HBM = pl.BlockSpec(memory_space=pltpu.HBM)
SM = pl.BlockSpec(memory_space=pltpu.SMEM)
F32, BF16 = jnp.float32, jnp.bfloat16
LANES = 128


def dot(a, b, dims):
    return lax.dot_general(a, b, (dims, ((), ())), preferred_element_type=F32)


NN, NT, TN = ((1,), (0,)), ((1,), (1,)), ((0,), (0,))


def pieces(x):
    hi = x.astype(BF16)
    return hi, (x - hi.astype(F32)).astype(BF16)


def halo_kernel(n, data, tmpl, wide, lsem, ssem, rsem):
    v = lax.axis_index("vert")
    ns, nt, own = data.shape
    width = (wide.shape[1] - own) // 2
    barrier = pltpu.get_barrier_semaphore()
    lower, upper = v > 0, v < n - 1

    def greet(other):
        pl.semaphore_signal(barrier, inc=1, device_id={"vert": other}, device_id_type=MESH)

    def rows(i):
        return pl.ds(i * nt, nt)

    def src(i, cols):
        return data.at[i, :, cols] if i < ns else tmpl.at[:, cols]

    pl.when(lower)(lambda: greet(v - 1))
    pl.when(upper)(lambda: greet(v + 1))
    mine = [
        pltpu.make_async_copy(
            src(i, pl.ds(0, own)), wide.at[rows(i), pl.ds(width, own)], lsem.at[i])
        for i in range(ns + 1)
    ]
    for c in mine:
        c.start()
    pl.semaphore_wait(barrier, jnp.minimum(v, 1) + jnp.minimum(n - 1 - v, 1))

    def copies(up):
        cols = pl.ds(own - width, width) if up else pl.ds(0, width)
        dst = pl.ds(0, width) if up else pl.ds(width + own, width)
        to = {"vert": v + 1 if up else v - 1}
        k = 0 if up else ns + 1
        return [
            pltpu.make_async_remote_copy(
                src(i, cols), wide.at[rows(i), dst], ssem.at[k + i], rsem.at[k + i],
                device_id=to, device_id_type=MESH)
            for i in range(ns + 1)
        ]

    def start(up):
        for c in copies(up):
            c.start()

    def sent(up):
        for c in copies(up):
            c.wait_send()

    def received(up):
        for c in copies(up):
            c.wait_recv()

    def blank(at):
        wide[:, pl.ds(at, width)] = jnp.zeros((wide.shape[0], width), wide.dtype)

    pl.when(upper)(lambda: start(True))
    pl.when(lower)(lambda: start(False))
    pl.when(jnp.logical_not(lower))(lambda: blank(0))
    pl.when(jnp.logical_not(upper))(lambda: blank(width + own))
    for c in mine:
        c.wait()
    pl.when(upper)(lambda: sent(True))
    pl.when(lower)(lambda: sent(False))
    pl.when(lower)(lambda: received(True))
    pl.when(upper)(lambda: received(False))


def halos(data, template, n, width):
    ns, nt, own = data.shape
    sem = pltpu.SemaphoreType.DMA
    return pl.pallas_call(
        functools.partial(halo_kernel, n),
        out_shape=jax.ShapeDtypeStruct(((ns + 1) * nt, own + 2 * width), data.dtype),
        in_specs=[HBM, HBM],
        out_specs=VM,
        scratch_shapes=[sem((ns + 1,)), sem((2 * ns + 2,)), sem((2 * ns + 2,))],
        compiler_params=pltpu.CompilerParams(
            collective_id=0, has_side_effects=True, vmem_limit_bytes=8 << 20),
        name="halo",
    )(*(pltpu.with_memory_space_constraint(a, pltpu.HBM) for a in (data, template)))


def align_kernel(ns, unroll, cen, nb, wide, aligned, partial, acc, xbuf, zbuf, ybuf, abuf, sem):
    lights, width = nb.shape
    nt, own = partial.shape
    tiles = own // LANES
    groups = lights // unroll
    lane = lax.broadcasted_iota(jnp.int32, (1, LANES), 1)

    def rows(i):
        return pl.ds(i * nt, nt)

    ones = jnp.ones((16, width), BF16)
    none = jnp.zeros((16, width), BF16)

    nil = [jnp.zeros((1, 1), F32)]

    def window(c):
        local = lax.rem(cen[c], own)
        base = pl.multiple_of(lax.div(local, LANES) * LANES, LANES)
        target = nb[pl.ds(c, 1), :] + width
        pick = (lax.broadcasted_iota(jnp.int32, (2 * LANES, width), 0) == target)
        return base, local - base, pick.astype(F32).astype(BF16)

    def gather(g):
        for u in range(unroll):
            base, off, pick = window(g * unroll + u)
            back = lax.rem(LANES - off, LANES)
            kept = lane < LANES - off
            x = []
            for i in range(ns + 1):
                p, q, r = (
                    pltpu.roll(wide[rows(i), pl.ds(base + k * LANES, LANES)], back, 1)
                    for k in range(3))
                seen = jnp.concatenate([jnp.where(kept, p, q), jnp.where(kept, q, r)], axis=1)
                got = dot(seen, pick, NN)
                nil[0] = jnp.minimum(jnp.abs(got[0:1, 0:1]), 0.0)
                x.append(got.astype(BF16))
                yield
            m = x.pop()
            for i in range(ns):
                xbuf[lax.rem(g, 3), u * ns + i] = x[i]
            both = dot(m, jnp.concatenate(x, axis=1), TN)
            for i in range(ns):
                z = both[:, i * width:(i + 1) * width]
                norm = jnp.sum(z * z, axis=(0, 1), keepdims=True)
                zbuf[lax.rem(g, 2), u * ns + i] = z * (1.0 / jnp.sqrt(norm + 1e-06))
            yield

    def iterate(g):
        zs = [zbuf[lax.rem(g, 2), k] for k in range(unroll * ns)]
        for step in range(NS_STEPS):
            grams = []
            for z in zs:
                zh, zl = pieces(z)
                a = jnp.concatenate([zh, zl], axis=1)
                b = jnp.concatenate(
                    [jnp.concatenate([zh, zh], axis=1), jnp.concatenate([zl, zl], axis=1)], axis=0)
                p = dot(a, b, NT)
                grams.append((p[:, :width] + p[:, width:], zh, zl))
                yield
            nxt = []
            for z, (gram, zh, zl) in zip(zs, grams):
                gh, gl = pieces(gram)
                a = jnp.concatenate([gh, gl], axis=1)
                b = jnp.concatenate([zh, zl], axis=1)
                p = dot(a, jnp.concatenate([b, b], axis=0), NN)
                nxt.append(1.5 * z - 0.5 * (p[:, :width] + p[:, width:]))
                yield
            zs = nxt
        for k, z in enumerate(zs):
            ybuf[lax.rem(g, 2), k] = jnp.concatenate(pieces(z), axis=1)

    def scatter(g):
        for u in range(unroll):
            base, off, pick = window(g * unroll + u)
            parts = []
            for i in range(ns):
                x = xbuf[lax.rem(g, 3), u * ns + i]
                turned = dot(
                    jnp.concatenate([x, x], axis=1), ybuf[lax.rem(g, 2), u * ns + i], NT)
                parts.append(jnp.concatenate(pieces(turned), axis=1))
                yield
            parts[-1] = jnp.concatenate([parts[-1], jnp.concatenate([ones, none], axis=1)], axis=0)
            twice = jnp.concatenate([pick, pick], axis=1)
            inside = lane >= off
            for i in range(ns):
                spread = dot(parts[i], twice, NT)
                at = pl.ds(i * nt, spread.shape[0])
                p, q = (pltpu.roll(spread[:, k * LANES:(k + 1) * LANES], off, 1) for k in range(2))
                acc[at, pl.ds(base, LANES)] += jnp.where(inside, p, 0.0)
                acc[at, pl.ds(base + LANES, LANES)] += jnp.where(inside, q, p)
                acc[at, pl.ds(base + 2 * LANES, LANES)] += jnp.where(inside, 0.0, q)
                yield

    def together(*works):
        works = [[w, n, 0] for w, n in works]
        while works:
            w = min(works, key=lambda w: (w[2] + 0.5) / w[1])
            w[2] += 1
            if next(w[0], works) is works:
                works.remove(w)

    def zeroing():
        for k in range(0, ns * nt + 16, 16):
            acc[k:k + 16, :] = jnp.broadcast_to(nil[0], (16, acc.shape[1]))
            yield

    def gathering(g):
        return gather(g), unroll * (ns + 2)

    def iterating(g):
        return iterate(g), 2 * NS_STEPS * unroll * ns

    def scattering(g):
        return scatter(g), unroll * 2 * ns

    def body(g, _):
        together(scattering(g - 1), iterating(g), gathering(g + 1))
        return 0

    together(gathering(0), (zeroing(), (ns * nt + 16) // 16))
    together(iterating(0), gathering(1))
    lax.fori_loop(1, groups - 1, body, 0)
    together(scattering(groups - 2), iterating(groups - 1))
    together(scattering(groups - 1))
    stores = []
    for t in range(1, tiles - 1):
        src = pl.ds((t + 1) * LANES, LANES)
        dst = pl.ds(t * LANES, LANES)
        inv = 1.0 / jnp.maximum(acc[pl.ds(ns * nt, 1), src], 1.0)
        total = None
        for i in range(ns):
            mapped = acc[rows(i), src] * inv
            abuf[i, :, dst] = mapped.astype(BF16)
            total = mapped if total is None else total + mapped
        partial[:, pl.ds((t - 1) * LANES, LANES)] = total
        if t % 2 == 0:
            at = pl.ds((t - 1) * LANES, 2 * LANES)
            stores.append(pltpu.make_async_copy(
                abuf.at[:, :, at], aligned.at[:, :, at], sem.at[t // 2 - 1]))
            stores[-1].start()
    for c in stores:
        c.wait()


def align(centres, neighbours, wide, shape):
    ns, nt, own = shape
    width = neighbours.shape[1]
    return pl.pallas_call(
        functools.partial(align_kernel, ns, UNROLL),
        out_shape=(
            jax.ShapeDtypeStruct(shape, BF16),
            jax.ShapeDtypeStruct((nt, own), F32),
            jax.ShapeDtypeStruct((ns * nt + 16, wide.shape[1]), F32),
        ),
        in_specs=[SM, VM, VM],
        out_specs=(HBM, VM, VM),
        scratch_shapes=[
            pltpu.VMEM((3, UNROLL * ns, nt, width), BF16),
            pltpu.VMEM((2, UNROLL * ns, width, width), F32),
            pltpu.VMEM((2, UNROLL * ns, width, 2 * width), BF16),
            pltpu.VMEM(shape, BF16),
            pltpu.SemaphoreType.DMA((own // (2 * LANES) - 1,)),
        ],
        compiler_params=pltpu.CompilerParams(vmem_limit_bytes=24 << 20),
        name="align",
    )(centres, neighbours, wide)


NZ, NX, NY = 2, 4, 4
WIDTHS = (256, 256, 256, 256, 256, 256, 256, 256)
ORDER = (
    0, 1, 2, 3, 4, 5, 6, 7, 8, 9, 10, 11, 12, 13, 14, 15,
    17, 16, 18, 19, 20, 21, 22, 23, 25, 24, 26, 27, 28, 29, 30, 31,
    33, 32, 34, 35, 36, 37, 38, 39, 41, 40, 43, 42, 45, 44, 47, 46,
)
SENDS = 13


def reduce_kernel(n, ns, chunks, part, sums, out, edge_aligned, full, edge_part, edge_in,
                  tx, rx, ag, q1, r2, q2, zin,
                  ssem, rsem, esem):
    s, v = lax.axis_index("subj"), lax.axis_index("vert")
    nt, own = full.shape
    width = edge_in.shape[2]
    y, x, zh = lax.rem(s, NY), lax.rem(lax.div(s, NY), NX), lax.div(s, NX * NY)

    def place(zh, x, y):
        return {"subj": (zh * NX + x) * NY + y}

    def along(axis, by):
        if axis == 0:
            return place(zh, lax.rem(x + by + NX, NX), y)
        return place(zh, x, lax.rem(y + by + NY, NY))

    across = place(NZ - 1 - zh, x, y)
    barrier = pltpu.get_barrier_semaphore()
    lower, upper = v > 0, v < n - 1

    def greet(to):
        pl.semaphore_signal(barrier, inc=1, device_id=to, device_id_type=MESH)

    for to in [along(axis, by) for axis in range(2) for by in (1, 2, -1)] + [across]:
        greet(to)
    pl.when(lower)(lambda: greet({"vert": v - 1}))
    pl.when(upper)(lambda: greet({"vert": v + 1}))
    pl.semaphore_wait(barrier, 7 + jnp.minimum(v, 1) + jnp.minimum(n - 1 - v, 1))

    def edge_copy(up):
        k = 1 if up else 0
        cols = pl.ds(width + own, width) if up else pl.ds(0, width)
        return pltpu.make_async_remote_copy(
            sums.at[pl.ds(0, ns * nt + 8), cols], edge_in.at[k], esem.at[0, k], esem.at[1, k],
            device_id={"vert": v + 1 if up else v - 1}, device_id_type=MESH)

    def edge_start(up):
        edge_copy(up).start()

    def edge_sent(up):
        edge_copy(up).wait_send()

    def edge_got(up):
        edge_copy(up).wait_recv()

    def edge_blank(up):
        k = 1 if up else 0
        edge_in[k] = jnp.zeros(edge_in.shape[1:], F32)

    pl.when(upper)(lambda: edge_start(True))
    pl.when(lower)(lambda: edge_start(False))
    pl.when(jnp.logical_not(lower))(lambda: edge_blank(True))
    pl.when(jnp.logical_not(upper))(lambda: edge_blank(False))

    def edges():
        pl.when(lower)(lambda: edge_got(True))
        pl.when(upper)(lambda: edge_got(False))
        for side in range(2):
            k = 1 - side
            at = pl.ds(width if side == 0 else own, width)
            count = sums[pl.ds(ns * nt, 1), at] + edge_in[k, pl.ds(ns * nt, 1), :]
            inv = 1.0 / jnp.maximum(count, 1.0)
            total = None
            for i in range(ns):
                mine = pl.ds(i * nt, nt)
                mapped = (sums[mine, at] + edge_in[k, mine, :]) * inv
                edge_aligned[side, i] = mapped.astype(BF16)
                total = mapped if total is None else total + mapped
            edge_part[:, side * width:(side + 1) * width] = total

    sends = []

    def remote(c, k, a, b, to):
        return pltpu.make_async_remote_copy(
            a, b, ssem.at[c, k], rsem.at[c, k], device_id=to, device_id_type=MESH)

    def go(*what):
        d = remote(*what)
        d.start()
        sends.append(d)

    hops = (2, 1, -1)
    tall = 16
    big, mid = nt // 4, nt // 16

    def spots(unit, size):
        return [
            (slice(i, i + tall), slice(j, j + LANES))
            for i in range(0, unit, tall) for j in range(0, size, LANES)]

    def encode(x, ref, index):
        parts = [x[i, j] for i, j in spots(*x.shape)]
        peak = functools.reduce(jnp.maximum, [jnp.abs(t) for t in parts])
        power = jnp.ceil(jnp.log2(jnp.maximum(peak, 1e-30)))
        scale = jnp.exp2(15.0 - power)
        for k, t in enumerate(parts):
            code = jnp.clip(jnp.round(t * scale), -32767.0, 32767.0)
            ref[(*index, k)] = code.astype(jnp.int32).astype(jnp.int16)
        ref[(*index, len(parts))] = power.astype(jnp.int32).astype(jnp.int16)

    def decode(ref, index, count):
        power = ref[(*index, count)].astype(jnp.int32).astype(F32)
        scale = jnp.exp2(power - 15.0)
        return [ref[(*index, k)].astype(jnp.int32).astype(F32) * scale for k in range(count)]

    def rs_stages(c, first, axis, p, src, cols, unit, r, dst):
        def slot(k):
            return pl.ds(k * unit, unit)

        def start():
            for k, by in enumerate(hops):
                ref, at, cc = src(lax.rem(p + by + 4, 4))
                go(c, first + k, ref.at[at, cc], r.at[slot(k), cols], along(axis, by))

        def end():
            for k in (1, 2, 0):
                b = r.at[slot(k), cols]
                remote(c, first + k, b, b, along(axis, 1)).wait_recv()
            ref, at, cc = src(p)
            dst[:, cols] = (ref[at, cc] + r[slot(0), cols]) + (r[slot(1), cols] + r[slot(2), cols])

        return start, end

    def ag_stages(c, first, axis, p, piece):
        def start():
            for k, by in enumerate(hops):
                go(c, first + k, piece(p), piece(p), along(axis, by))

        def end():
            for k, by in enumerate(hops):
                b = piece(lax.rem(p - by + 4, 4))
                remote(c, first + k, b, b, along(axis, 1)).wait_recv()

        return start, end

    def coded_rs(c, axis, p, src, col, size):
        places = spots(big, size)

        def start():
            for k, by in enumerate(hops):
                ref, at, cc = src(lax.rem(p + by + 4, 4))
                encode(ref[at, cc], tx, (c, k))
                go(c, k, tx.at[c, k], rx.at[c, k], along(axis, by))

        def end():
            for k in (1, 2, 0):
                remote(c, k, rx.at[c, k], rx.at[c, k], along(axis, 1)).wait_recv()
            far, one, two = (decode(rx, (c, k), len(places)) for k in range(3))
            ref, at, cc = src(p)
            mine = ref[at, cc]
            for (i, j), f, a, b in zip(places, far, one, two):
                q1[i, col + j.start:col + j.stop] = (mine[i, j] + f) + (a + b)

        return start, end

    def coded_ag(c, axis, p, col, size, edge):
        places = spots(big, size)

        def start():
            encode(full[pl.ds(pl.multiple_of(p * big, big), big), pl.ds(col, size)], ag, (c, p))
            for k, by in enumerate(hops):
                go(c, 10 + k, ag.at[c, p], ag.at[c, p], along(axis, by))

        def end():
            for k, by in enumerate(hops):
                b = ag.at[c, lax.rem(p - by + 4, 4)]
                remote(c, 10 + k, b, b, along(axis, 1)).wait_recv()
            for q in range(4):
                for (i, j), t in zip(places, decode(ag, (c, q), len(places))):
                    to = (own - width if j.start else 0) if edge else col + width + j.start
                    out[q * big + i.start:q * big + i.stop, to:to + LANES] = t

        return start, end


    def chunk(c, col, size, order):
        edge = order is None
        first = 1 if edge else order
        second = 1 - first
        pos = (x, y)
        p1, p2 = pos[first], pos[second]
        cols = pl.ds(col, size)

        def rows(q, unit, base=0):
            return pl.ds(pl.multiple_of(base + q * unit, unit), unit)

        def src1(q):
            if edge:
                return edge_part, rows(q, big), pl.ds(0, size)
            return part, rows(q, big), cols

        def src2(q):
            return q1, rows(q, mid), cols

        a1, c1 = coded_rs(c, first, p1, src1, col, size)
        a2, c2 = rs_stages(c, 3, second, p2, src2, cols, mid, r2, q2)
        base = p1 * big
        g2, i2 = ag_stages(c, 7, second, p2, lambda q: full.at[rows(q, mid, base), cols])
        g1, i1 = coded_ag(c, first, p1, col, size, edge)
        z = c, 6, q2.at[:, cols], zin.at[:, cols], across

        def stage0():
            if edge:
                edges()
            a1()

        def stage1():
            c1()
            a2()

        def stage2():
            c2()
            go(*z)

        def stage3():
            remote(*z).wait_recv()
            full[rows(p2, mid, base), cols] = (q2[:, cols] + zin[:, cols]) * (
                1.0 / (ns * NZ * NX * NY))
            g2()

        def stage4():
            i2()
            g1()

        return stage0, stage1, stage2, stage3, stage4, i1

    work = [chunk(c, *spec) for c, spec in enumerate(chunks)]
    for code in ORDER:
        work[code % len(work)][code // len(work)]()
    for d in sends:
        d.wait_send()
    pl.when(upper)(lambda: edge_sent(True))
    pl.when(lower)(lambda: edge_sent(False))


def reduce(partial, sums, ns, width, n):
    nt, own = partial.shape
    count = len(WIDTHS)
    chunks = tuple(
        (sum(WIDTHS[:k]), WIDTHS[k], k % 2 if k < count - 1 else None) for k in range(count))

    def rows(k):
        return pltpu.VMEM((k, own), F32)

    tiles = (nt // 4) * max(WIDTHS) // (16 * LANES) + 1

    def codes(k):
        return pltpu.VMEM((count, k, tiles, 16, LANES), jnp.int16)

    sem = pltpu.SemaphoreType.DMA
    return pl.pallas_call(
        functools.partial(reduce_kernel, n, ns, chunks),
        out_shape=(
            jax.ShapeDtypeStruct((nt, own), F32),
            jax.ShapeDtypeStruct((2, ns, nt, width), BF16),
        ),
        in_specs=[VM] * 2,
        out_specs=(VM, VM),
        scratch_shapes=[
            rows(nt),
            pltpu.VMEM((nt, 2 * width), F32),
            pltpu.VMEM((2, ns * nt + 8, width), F32),
            codes(3), codes(3), codes(4),
            rows(nt // 4), rows(3 * nt // 16), rows(nt // 16), rows(nt // 16),
            sem((count, SENDS)), sem((count, SENDS)), sem((2, 2)),
        ],
        compiler_params=pltpu.CompilerParams(
            collective_id=1, has_side_effects=True, vmem_limit_bytes=28 << 20),
        name="reduce",
    )(partial, sums)


def finish_kernel(aligned_in, edge_aligned, template_in, aligned, template, sem):
    own = aligned.shape[2]
    width = edge_aligned.shape[3]
    stores = [pltpu.make_async_copy(template_in, template, sem.at[2])]
    for side in range(2):
        cols = pl.ds(0 if side == 0 else own - width, width)
        stores.append(pltpu.make_async_copy(
            edge_aligned.at[side], aligned.at[:, :, cols], sem.at[side]))
    for c in stores:
        c.start()
    for c in stores:
        c.wait()


def finish(aligned, edge_aligned, template):
    return pl.pallas_call(
        finish_kernel,
        out_shape=(
            jax.ShapeDtypeStruct(aligned.shape, aligned.dtype),
            jax.ShapeDtypeStruct(template.shape, template.dtype),
        ),
        in_specs=[HBM, VM, VM],
        out_specs=(HBM, HBM),
        scratch_shapes=[pltpu.SemaphoreType.DMA((3,))],
        input_output_aliases={0: 0},
        compiler_params=pltpu.CompilerParams(vmem_limit_bytes=8 << 20),
        name="finish",
    )(aligned, edge_aligned, template)


def local(n, data, template, centres, neighbours):
    width = neighbours.shape[1]
    wide = halos(data, template, n, width)
    aligned, partial, sums = align(centres, neighbours, wide, data.shape)
    new_template, edge_aligned = reduce(partial, sums, data.shape[0], width, n)
    return finish(aligned, edge_aligned, new_template)


def solution(mesh):
    in_specs = (P("subj", None, "vert"), P(None, "vert"), P("vert"), P("vert", None))
    out_specs = (P("subj", None, "vert"), P(None, "vert"))
    return jax.shard_map(
        functools.partial(local, mesh.shape["vert"]), mesh=mesh,
        in_specs=in_specs, out_specs=out_specs, check_vma=False)
```

```python
import functools

import jax
import jax.numpy as jnp
from jax import lax
from jax.experimental import pallas as pl
from jax.experimental.pallas import tpu as pltpu
from jax.sharding import PartitionSpec as P

NS_STEPS = 4
UNROLL = 4
MESH = pl.DeviceIdType.MESH
ANY = pl.BlockSpec(memory_space=pl.ANY)
VM = pl.BlockSpec(memory_space=pltpu.VMEM)
HBM = pl.BlockSpec(memory_space=pltpu.HBM)
SM = pl.BlockSpec(memory_space=pltpu.SMEM)
F32, BF16 = jnp.float32, jnp.bfloat16
LANES = 128


def dot(a, b, dims):
    return lax.dot_general(a, b, (dims, ((), ())), preferred_element_type=F32)


NN, NT, TN = ((1,), (0,)), ((1,), (1,)), ((0,), (0,))


def pieces(x):
    hi = x.astype(BF16)
    return hi, (x - hi.astype(F32)).astype(BF16)


def halo_kernel(n, data, tmpl, wide, lsem, ssem, rsem):
    v = lax.axis_index("vert")
    ns, nt, own = data.shape
    width = (wide.shape[1] - own) // 2
    barrier = pltpu.get_barrier_semaphore()
    lower, upper = v > 0, v < n - 1

    def greet(other):
        pl.semaphore_signal(barrier, inc=1, device_id={"vert": other}, device_id_type=MESH)

    def rows(i):
        return pl.ds(i * nt, nt)

    def src(i, cols):
        return data.at[i, :, cols] if i < ns else tmpl.at[:, cols]

    pl.when(lower)(lambda: greet(v - 1))
    pl.when(upper)(lambda: greet(v + 1))
    mine = [
        pltpu.make_async_copy(
            src(i, pl.ds(0, own)), wide.at[rows(i), pl.ds(width, own)], lsem.at[i])
        for i in range(ns + 1)
    ]
    for c in mine:
        c.start()
    pl.semaphore_wait(barrier, jnp.minimum(v, 1) + jnp.minimum(n - 1 - v, 1))

    def copies(up):
        cols = pl.ds(own - width, width) if up else pl.ds(0, width)
        dst = pl.ds(0, width) if up else pl.ds(width + own, width)
        to = {"vert": v + 1 if up else v - 1}
        k = 0 if up else ns + 1
        return [
            pltpu.make_async_remote_copy(
                src(i, cols), wide.at[rows(i), dst], ssem.at[k + i], rsem.at[k + i],
                device_id=to, device_id_type=MESH)
            for i in range(ns + 1)
        ]

    def start(up):
        for c in copies(up):
            c.start()

    def sent(up):
        for c in copies(up):
            c.wait_send()

    def received(up):
        for c in copies(up):
            c.wait_recv()

    def blank(at):
        wide[:, pl.ds(at, width)] = jnp.zeros((wide.shape[0], width), wide.dtype)

    pl.when(upper)(lambda: start(True))
    pl.when(lower)(lambda: start(False))
    pl.when(jnp.logical_not(lower))(lambda: blank(0))
    pl.when(jnp.logical_not(upper))(lambda: blank(width + own))
    for c in mine:
        c.wait()
    pl.when(upper)(lambda: sent(True))
    pl.when(lower)(lambda: sent(False))
    pl.when(lower)(lambda: received(True))
    pl.when(upper)(lambda: received(False))


def halos(data, template, n, width):
    ns, nt, own = data.shape
    sem = pltpu.SemaphoreType.DMA
    return pl.pallas_call(
        functools.partial(halo_kernel, n),
        out_shape=jax.ShapeDtypeStruct(((ns + 1) * nt, own + 2 * width), data.dtype),
        in_specs=[HBM, HBM],
        out_specs=VM,
        scratch_shapes=[sem((ns + 1,)), sem((2 * ns + 2,)), sem((2 * ns + 2,))],
        compiler_params=pltpu.CompilerParams(
            collective_id=0, has_side_effects=True, vmem_limit_bytes=8 << 20),
        name="halo",
    )(*(pltpu.with_memory_space_constraint(a, pltpu.HBM) for a in (data, template)))


def align_kernel(ns, unroll, cen, nb, wide, aligned, partial, acc, xbuf, zbuf, ybuf, abuf, sem):
    lights, width = nb.shape
    nt, own = partial.shape
    tiles = own // LANES
    groups = lights // unroll
    lane = lax.broadcasted_iota(jnp.int32, (1, LANES), 1)

    def rows(i):
        return pl.ds(i * nt, nt)

    ones = jnp.ones((16, width), BF16)
    none = jnp.zeros((16, width), BF16)

    nil = [jnp.zeros((1, 1), F32)]

    def window(c):
        local = lax.rem(cen[c], own)
        base = pl.multiple_of(lax.div(local, LANES) * LANES, LANES)
        target = nb[pl.ds(c, 1), :] + width
        pick = (lax.broadcasted_iota(jnp.int32, (2 * LANES, width), 0) == target)
        return base, local - base, pick.astype(F32).astype(BF16)

    def gather(g):
        for u in range(unroll):
            base, off, pick = window(g * unroll + u)
            back = lax.rem(LANES - off, LANES)
            kept = lane < LANES - off
            x = []
            for i in range(ns + 1):
                p, q, r = (
                    pltpu.roll(wide[rows(i), pl.ds(base + k * LANES, LANES)], back, 1)
                    for k in range(3))
                seen = jnp.concatenate([jnp.where(kept, p, q), jnp.where(kept, q, r)], axis=1)
                got = dot(seen, pick, NN)
                nil[0] = jnp.minimum(jnp.abs(got[0:1, 0:1]), 0.0)
                x.append(got.astype(BF16))
                yield
            m = x.pop()
            for i in range(ns):
                xbuf[lax.rem(g, 3), u * ns + i] = x[i]
            both = dot(m, jnp.concatenate(x, axis=1), TN)
            for i in range(ns):
                z = both[:, i * width:(i + 1) * width]
                norm = jnp.sum(z * z, axis=(0, 1), keepdims=True)
                zbuf[lax.rem(g, 2), u * ns + i] = z * (1.0 / jnp.sqrt(norm + 1e-06))
            yield

    def iterate(g):
        zs = [zbuf[lax.rem(g, 2), k] for k in range(unroll * ns)]
        for step in range(NS_STEPS):
            grams = []
            for z in zs:
                zh, zl = pieces(z)
                a = jnp.concatenate([zh, zl], axis=1)
                b = jnp.concatenate(
                    [jnp.concatenate([zh, zh], axis=1), jnp.concatenate([zl, zl], axis=1)], axis=0)
                p = dot(a, b, NT)
                grams.append((p[:, :width] + p[:, width:], zh, zl))
                yield
            nxt = []
            for z, (gram, zh, zl) in zip(zs, grams):
                gh, gl = pieces(gram)
                a = jnp.concatenate([gh, gl], axis=1)
                b = jnp.concatenate([zh, zl], axis=1)
                p = dot(a, jnp.concatenate([b, b], axis=0), NN)
                nxt.append(1.5 * z - 0.5 * (p[:, :width] + p[:, width:]))
                yield
            zs = nxt
        for k, z in enumerate(zs):
            ybuf[lax.rem(g, 2), k] = jnp.concatenate(pieces(z), axis=1)

    def scatter(g):
        for u in range(unroll):
            base, off, pick = window(g * unroll + u)
            parts = []
            for i in range(ns):
                x = xbuf[lax.rem(g, 3), u * ns + i]
                turned = dot(
                    jnp.concatenate([x, x], axis=1), ybuf[lax.rem(g, 2), u * ns + i], NT)
                parts.append(jnp.concatenate(pieces(turned), axis=1))
                yield
            parts[-1] = jnp.concatenate([parts[-1], jnp.concatenate([ones, none], axis=1)], axis=0)
            twice = jnp.concatenate([pick, pick], axis=1)
            inside = lane >= off
            for i in range(ns):
                spread = dot(parts[i], twice, NT)
                at = pl.ds(i * nt, spread.shape[0])
                p, q = (pltpu.roll(spread[:, k * LANES:(k + 1) * LANES], off, 1) for k in range(2))
                acc[at, pl.ds(base, LANES)] += jnp.where(inside, p, 0.0)
                acc[at, pl.ds(base + LANES, LANES)] += jnp.where(inside, q, p)
                acc[at, pl.ds(base + 2 * LANES, LANES)] += jnp.where(inside, 0.0, q)
                yield

    def together(*works):
        works = [[w, n, 0] for w, n in works]
        while works:
            w = min(works, key=lambda w: (w[2] + 0.5) / w[1])
            w[2] += 1
            if next(w[0], works) is works:
                works.remove(w)

    def zeroing():
        for k in range(0, ns * nt + 16, 16):
            acc[k:k + 16, :] = jnp.broadcast_to(nil[0], (16, acc.shape[1]))
            yield

    def gathering(g):
        return gather(g), unroll * (ns + 2)

    def iterating(g):
        return iterate(g), 2 * NS_STEPS * unroll * ns

    def scattering(g):
        return scatter(g), unroll * 2 * ns

    def body(g, _):
        together(scattering(g - 1), iterating(g), gathering(g + 1))
        return 0

    together(gathering(0), (zeroing(), (ns * nt + 16) // 16))
    together(iterating(0), gathering(1))
    lax.fori_loop(1, groups - 1, body, 0)
    together(scattering(groups - 2), iterating(groups - 1))
    together(scattering(groups - 1))
    stores = []
    for t in range(1, tiles - 1):
        src = pl.ds((t + 1) * LANES, LANES)
        dst = pl.ds(t * LANES, LANES)
        inv = 1.0 / jnp.maximum(acc[pl.ds(ns * nt, 1), src], 1.0)
        total = None
        for i in range(ns):
            mapped = acc[rows(i), src] * inv
            abuf[i, :, dst] = mapped.astype(BF16)
            total = mapped if total is None else total + mapped
        partial[:, pl.ds((t - 1) * LANES, LANES)] = total
        if t % 2 == 0:
            at = pl.ds((t - 1) * LANES, 2 * LANES)
            stores.append(pltpu.make_async_copy(
                abuf.at[:, :, at], aligned.at[:, :, at], sem.at[t // 2 - 1]))
            stores[-1].start()
    for c in stores:
        c.wait()


def align(centres, neighbours, wide, shape):
    ns, nt, own = shape
    width = neighbours.shape[1]
    return pl.pallas_call(
        functools.partial(align_kernel, ns, UNROLL),
        out_shape=(
            jax.ShapeDtypeStruct(shape, BF16),
            jax.ShapeDtypeStruct((nt, own), F32),
            jax.ShapeDtypeStruct((ns * nt + 16, wide.shape[1]), F32),
        ),
        in_specs=[SM, VM, VM],
        out_specs=(HBM, VM, VM),
        scratch_shapes=[
            pltpu.VMEM((3, UNROLL * ns, nt, width), BF16),
            pltpu.VMEM((2, UNROLL * ns, width, width), F32),
            pltpu.VMEM((2, UNROLL * ns, width, 2 * width), BF16),
            pltpu.VMEM(shape, BF16),
            pltpu.SemaphoreType.DMA((own // (2 * LANES) - 1,)),
        ],
        compiler_params=pltpu.CompilerParams(vmem_limit_bytes=24 << 20),
        name="align",
    )(centres, neighbours, wide)


NZ, NX, NY = 2, 4, 4
WIDTHS = (256, 256, 256, 256, 256, 256, 256, 256)
ORDER = (
    0, 1, 2, 3, 4, 5, 6, 7, 8, 9, 10, 11, 12, 13, 14, 15,
    17, 16, 19, 18, 21, 20, 23, 22, 25, 24, 27, 26, 29, 28, 31, 30,
    33, 32, 35, 34, 37, 36, 39, 38, 40, 41, 42, 43, 44, 45, 46, 47,
)
SENDS = 13


def reduce_kernel(n, ns, chunks, part, sums, out, edge_aligned, full, edge_part, edge_in,
                  tx, rx, ag, q1, r2, q2, zin,
                  ssem, rsem, esem):
    s, v = lax.axis_index("subj"), lax.axis_index("vert")
    nt, own = full.shape
    width = edge_in.shape[2]
    y, x, zh = lax.rem(s, NY), lax.rem(lax.div(s, NY), NX), lax.div(s, NX * NY)

    def place(zh, x, y):
        return {"subj": (zh * NX + x) * NY + y}

    def along(axis, by):
        if axis == 0:
            return place(zh, lax.rem(x + by + NX, NX), y)
        return place(zh, x, lax.rem(y + by + NY, NY))

    across = place(NZ - 1 - zh, x, y)
    barrier = pltpu.get_barrier_semaphore()
    lower, upper = v > 0, v < n - 1

    def greet(to):
        pl.semaphore_signal(barrier, inc=1, device_id=to, device_id_type=MESH)

    for to in [along(axis, by) for axis in range(2) for by in (1, 2, -1)] + [across]:
        greet(to)
    pl.when(lower)(lambda: greet({"vert": v - 1}))
    pl.when(upper)(lambda: greet({"vert": v + 1}))
    pl.semaphore_wait(barrier, 7 + jnp.minimum(v, 1) + jnp.minimum(n - 1 - v, 1))

    def edge_copy(up):
        k = 1 if up else 0
        cols = pl.ds(width + own, width) if up else pl.ds(0, width)
        return pltpu.make_async_remote_copy(
            sums.at[pl.ds(0, ns * nt + 8), cols], edge_in.at[k], esem.at[0, k], esem.at[1, k],
            device_id={"vert": v + 1 if up else v - 1}, device_id_type=MESH)

    def edge_start(up):
        edge_copy(up).start()

    def edge_sent(up):
        edge_copy(up).wait_send()

    def edge_got(up):
        edge_copy(up).wait_recv()

    def edge_blank(up):
        k = 1 if up else 0
        edge_in[k] = jnp.zeros(edge_in.shape[1:], F32)

    pl.when(upper)(lambda: edge_start(True))
    pl.when(lower)(lambda: edge_start(False))
    pl.when(jnp.logical_not(lower))(lambda: edge_blank(True))
    pl.when(jnp.logical_not(upper))(lambda: edge_blank(False))

    def edges():
        pl.when(lower)(lambda: edge_got(True))
        pl.when(upper)(lambda: edge_got(False))
        for side in range(2):
            k = 1 - side
            at = pl.ds(width if side == 0 else own, width)
            count = sums[pl.ds(ns * nt, 1), at] + edge_in[k, pl.ds(ns * nt, 1), :]
            inv = 1.0 / jnp.maximum(count, 1.0)
            total = None
            for i in range(ns):
                mine = pl.ds(i * nt, nt)
                mapped = (sums[mine, at] + edge_in[k, mine, :]) * inv
                edge_aligned[side, i] = mapped.astype(BF16)
                total = mapped if total is None else total + mapped
            edge_part[:, side * width:(side + 1) * width] = total

    sends = []

    def remote(c, k, a, b, to):
        return pltpu.make_async_remote_copy(
            a, b, ssem.at[c, k], rsem.at[c, k], device_id=to, device_id_type=MESH)

    def go(*what):
        d = remote(*what)
        d.start()
        sends.append(d)

    hops = (2, 1, -1)
    tall = 16
    big, mid = nt // 4, nt // 16

    def spots(unit, size):
        return [
            (slice(i, i + tall), slice(j, j + LANES))
            for i in range(0, unit, tall) for j in range(0, size, LANES)]

    def encode(x, ref, index):
        parts = [x[i, j] for i, j in spots(*x.shape)]
        peak = functools.reduce(jnp.maximum, [jnp.abs(t) for t in parts])
        power = jnp.ceil(jnp.log2(jnp.maximum(peak, 1e-30)))
        scale = jnp.exp2(15.0 - power)
        for k, t in enumerate(parts):
            code = jnp.clip(jnp.round(t * scale), -32767.0, 32767.0)
            ref[(*index, k)] = code.astype(jnp.int32).astype(jnp.int16)
        ref[(*index, len(parts))] = power.astype(jnp.int32).astype(jnp.int16)

    def decode(ref, index, count):
        power = ref[(*index, count)].astype(jnp.int32).astype(F32)
        scale = jnp.exp2(power - 15.0)
        return [ref[(*index, k)].astype(jnp.int32).astype(F32) * scale for k in range(count)]

    def rs_stages(c, first, axis, p, src, cols, unit, r, dst):
        def slot(k):
            return pl.ds(k * unit, unit)

        def start():
            for k, by in enumerate(hops):
                ref, at, cc = src(lax.rem(p + by + 4, 4))
                go(c, first + k, ref.at[at, cc], r.at[slot(k), cols], along(axis, by))

        def end():
            for k in (1, 2, 0):
                b = r.at[slot(k), cols]
                remote(c, first + k, b, b, along(axis, 1)).wait_recv()
            ref, at, cc = src(p)
            dst[:, cols] = (ref[at, cc] + r[slot(0), cols]) + (r[slot(1), cols] + r[slot(2), cols])

        return start, end

    def ag_stages(c, first, axis, p, piece):
        def start():
            for k, by in enumerate(hops):
                go(c, first + k, piece(p), piece(p), along(axis, by))

        def end():
            for k, by in enumerate(hops):
                b = piece(lax.rem(p - by + 4, 4))
                remote(c, first + k, b, b, along(axis, 1)).wait_recv()

        return start, end

    def coded_rs(c, axis, p, src, col, size):
        places = spots(big, size)

        def start():
            for k, by in enumerate(hops):
                ref, at, cc = src(lax.rem(p + by + 4, 4))
                encode(ref[at, cc], tx, (c, k))
                go(c, k, tx.at[c, k], rx.at[c, k], along(axis, by))

        def end():
            for k in (1, 2, 0):
                remote(c, k, rx.at[c, k], rx.at[c, k], along(axis, 1)).wait_recv()
            far, one, two = (decode(rx, (c, k), len(places)) for k in range(3))
            ref, at, cc = src(p)
            mine = ref[at, cc]
            for (i, j), f, a, b in zip(places, far, one, two):
                q1[i, col + j.start:col + j.stop] = (mine[i, j] + f) + (a + b)

        return start, end

    def coded_ag(c, axis, p, col, size, edge):
        places = spots(big, size)

        def start():
            encode(full[pl.ds(pl.multiple_of(p * big, big), big), pl.ds(col, size)], ag, (c, p))
            for k, by in enumerate(hops):
                go(c, 10 + k, ag.at[c, p], ag.at[c, p], along(axis, by))

        def end():
            for k, by in enumerate(hops):
                b = ag.at[c, lax.rem(p - by + 4, 4)]
                remote(c, 10 + k, b, b, along(axis, 1)).wait_recv()
            for q in range(4):
                for (i, j), t in zip(places, decode(ag, (c, q), len(places))):
                    to = (own - width if j.start else 0) if edge else col + width + j.start
                    out[q * big + i.start:q * big + i.stop, to:to + LANES] = t

        return start, end


    def chunk(c, col, size, order):
        edge = order is None
        first = 1 if edge else order
        second = 1 - first
        pos = (x, y)
        p1, p2 = pos[first], pos[second]
        cols = pl.ds(col, size)

        def rows(q, unit, base=0):
            return pl.ds(pl.multiple_of(base + q * unit, unit), unit)

        def src1(q):
            if edge:
                return edge_part, rows(q, big), pl.ds(0, size)
            return part, rows(q, big), cols

        def src2(q):
            return q1, rows(q, mid), cols

        a1, c1 = coded_rs(c, first, p1, src1, col, size)
        a2, c2 = rs_stages(c, 3, second, p2, src2, cols, mid, r2, q2)
        base = p1 * big
        g2, i2 = ag_stages(c, 7, second, p2, lambda q: full.at[rows(q, mid, base), cols])
        g1, i1 = coded_ag(c, first, p1, col, size, edge)
        z = c, 6, q2.at[:, cols], zin.at[:, cols], across

        def stage0():
            if edge:
                edges()
            a1()

        def stage1():
            c1()
            a2()

        def stage2():
            c2()
            go(*z)

        def stage3():
            remote(*z).wait_recv()
            full[rows(p2, mid, base), cols] = (q2[:, cols] + zin[:, cols]) * (
                1.0 / (ns * NZ * NX * NY))
            g2()

        def stage4():
            i2()
            g1()

        return stage0, stage1, stage2, stage3, stage4, i1

    work = [chunk(c, *spec) for c, spec in enumerate(chunks)]
    for code in ORDER:
        work[code % len(work)][code // len(work)]()
    for d in sends:
        d.wait_send()
    pl.when(upper)(lambda: edge_sent(True))
    pl.when(lower)(lambda: edge_sent(False))


def reduce(partial, sums, ns, width, n):
    nt, own = partial.shape
    count = len(WIDTHS)
    chunks = tuple(
        (sum(WIDTHS[:k]), WIDTHS[k], k % 2 if k < count - 1 else None) for k in range(count))

    def rows(k):
        return pltpu.VMEM((k, own), F32)

    tiles = (nt // 4) * max(WIDTHS) // (16 * LANES) + 1

    def codes(k):
        return pltpu.VMEM((count, k, tiles, 16, LANES), jnp.int16)

    sem = pltpu.SemaphoreType.DMA
    return pl.pallas_call(
        functools.partial(reduce_kernel, n, ns, chunks),
        out_shape=(
            jax.ShapeDtypeStruct((nt, own), F32),
            jax.ShapeDtypeStruct((2, ns, nt, width), BF16),
        ),
        in_specs=[VM] * 2,
        out_specs=(VM, VM),
        scratch_shapes=[
            rows(nt),
            pltpu.VMEM((nt, 2 * width), F32),
            pltpu.VMEM((2, ns * nt + 8, width), F32),
            codes(3), codes(3), codes(4),
            rows(nt // 4), rows(3 * nt // 16), rows(nt // 16), rows(nt // 16),
            sem((count, SENDS)), sem((count, SENDS)), sem((2, 2)),
        ],
        compiler_params=pltpu.CompilerParams(
            collective_id=1, has_side_effects=True, vmem_limit_bytes=28 << 20),
        name="reduce",
    )(partial, sums)


def finish_kernel(aligned_in, edge_aligned, template_in, aligned, template, sem):
    own = aligned.shape[2]
    width = edge_aligned.shape[3]
    stores = [pltpu.make_async_copy(template_in, template, sem.at[2])]
    for side in range(2):
        cols = pl.ds(0 if side == 0 else own - width, width)
        stores.append(pltpu.make_async_copy(
            edge_aligned.at[side], aligned.at[:, :, cols], sem.at[side]))
    for c in stores:
        c.start()
    for c in stores:
        c.wait()


def finish(aligned, edge_aligned, template):
    return pl.pallas_call(
        finish_kernel,
        out_shape=(
            jax.ShapeDtypeStruct(aligned.shape, aligned.dtype),
            jax.ShapeDtypeStruct(template.shape, template.dtype),
        ),
        in_specs=[HBM, VM, VM],
        out_specs=(HBM, HBM),
        scratch_shapes=[pltpu.SemaphoreType.DMA((3,))],
        input_output_aliases={0: 0},
        compiler_params=pltpu.CompilerParams(vmem_limit_bytes=8 << 20),
        name="finish",
    )(aligned, edge_aligned, template)


def local(n, data, template, centres, neighbours):
    width = neighbours.shape[1]
    wide = halos(data, template, n, width)
    aligned, partial, sums = align(centres, neighbours, wide, data.shape)
    new_template, edge_aligned = reduce(partial, sums, data.shape[0], width, n)
    return finish(aligned, edge_aligned, new_template)


def solution(mesh):
    in_specs = (P("subj", None, "vert"), P(None, "vert"), P("vert"), P("vert", None))
    out_specs = (P("subj", None, "vert"), P(None, "vert"))
    return jax.shard_map(
        functools.partial(local, mesh.shape["vert"]), mesh=mesh,
        in_specs=in_specs, out_specs=out_specs, check_vma=False)
```
